32 devices in a mesh: segment: 2 (over x), rep: 16 (over z, y, core).
Axes of the slice: x: 2, y: 2, z: 4, core: 2. Of those that a mesh axis runs over, the one named last changes fastest.
Arguments:
- feature_maps: bfloat16 [256, 7, 7, 1024], P(('segment', 'rep')), may hold values from -6 to 6
- path_lists: int32 [1, 256, 1], P(None, ('segment', 'rep')), may hold values from 0 to 1; in each aligned block of 8 rows (0 to 7, 8 to 15, ..., all dimensions but the last counted through in order) at most 4 rows name the same one
- point_weight: bfloat16 [1, 2, 1024, 1024], P(None, 'segment'), may hold values from -0.1875 to 0.1875
- depth_kernel: float32 [1, 2, 25, 1024], P(None, 'segment'), may hold values from -1.8 to 1.8
- cotangent: bfloat16 [256, 7, 7, 1024], P(('segment', 'rep')), may hold values from -6 to 6
Outputs:
- final_maps: bfloat16 [256, 7, 7, 1024], P(('segment', 'rep'))
- input_grad: bfloat16 [256, 7, 7, 1024], P(('segment', 'rep'))
- point_grad: float32 [1, 2, 1024, 1024], P(None, 'segment', 'rep')
- depth_grad: float32 [1, 2, 25, 1024], P(None, 'segment')
The draws below stay inside these ranges and needn't reach their ends.
Inputs may be any that keep to these rules, and one draw needn't show every extreme that they name: `path_lists`: in each layer, among the 8 samples of one device no operator is chosen by more than 4 samples.
All inputs are finite; a program needn't handle non-finite values.
Results may differ from the reference program's by a relative error of at most 0.0032.
Values may be sent and summed in bfloat16 or wider, within the bound.
No kernel may reach another device: no remote copies, remote signals or barrier semaphores. Data moves between devices by JAX's collectives and lax.ppermute only.
A program may use at most 128 MiB of HBM per device.

```python
import math
import jax
import jax.numpy as jnp
import numpy as np
from jax import lax

C = 1024
SIDE = 7
SMP_DEV = 8
LAYERS = 1
TAPS = 25
OPS = 2
CAP = 4
SAMPLES = 256


def steps_of(rng, extent, split, smallest, largest):
    loudness = 1.0
    for dim, blocks in split:
        heights = jax.random.uniform(jax.random.fold_in(jax.random.fold_in(rng, 6), dim), (blocks,), jnp.float32, smallest / len(split), largest / len(split))
        loudness = loudness * jnp.repeat(jnp.exp(heights), extent[dim] // blocks).reshape((-1,) + (1,) * (len(extent) - 1 - dim))
    return loudness


def routed_block(own_key, own, number, rows, number_of, top, limit, skew):
    sequence = jax.random.permutation(own_key, number_of)
    heavy_load, usual = load_shares(number_of, rows * top, limit, skew, True), load_shares(number_of, rows * top, limit, skew, False)
    places = jnp.arange(number_of)

    def named(sizes, offset_by):
        used = int((sizes > 0).sum())
        fixed = max(1, used // 4)
        passed = fixed + (places - fixed + offset_by * (used - fixed)) % max(1, number_of - fixed)
        return jnp.zeros((number_of,), jnp.int32).at[sequence[jnp.where(places < fixed, places, passed)]].set(jnp.asarray(sizes, jnp.int32))

    sizes = jnp.where(number % 4 == 0, named(heavy_load, number // 4), named(usual, number - number // 4 - 1))
    mixed = jax.random.permutation(jax.random.fold_in(own, 3), number_of)
    source_of, taker = mixed[0:number_of // 2 * 2:2], mixed[1:number_of // 2 * 2:2]
    room = jnp.minimum(sizes[source_of] - 1, limit - sizes[taker]) // 2
    room = jnp.where((source_of == sequence[0]) | (taker == sequence[0]) | (sizes[taker] == 0), 0, jnp.maximum(room, 0))
    passed = jax.random.randint(jax.random.fold_in(own, 4), (number_of // 2,), 0, 1 << 20) % (room + 1)
    sizes = sizes.at[source_of].add(-passed).at[taker].add(passed)
    labels = jnp.searchsorted(jnp.cumsum(sizes), jnp.arange(rows * top), side="right").astype(jnp.int32)
    listing = labels.reshape(top, rows).T
    listing = listing[jax.random.permutation(jax.random.fold_in(own, 1), rows)]
    offset_by = jax.random.randint(jax.random.fold_in(own, 2), (rows, 1), 0, top)
    return jnp.take_along_axis(listing, (jnp.arange(top)[None, :] + offset_by) % top, axis=1)


def load_shares(count, total, most, slope, full):
    portions = [(1 << 20) // math.isqrt(rank ** slope) + 1 for rank in range(1, count + 1)]
    largest = most if full else min(most, max(-(-total // count), total * portions[0] // sum(portions)))
    least = 1 if total - largest >= count - 1 else 0
    holding, surplus = [largest] + [least] * (count - 1), total - largest - least * (count - 1)
    while surplus > 0:
        free = [i for i in range(1, count) if holding[i] < largest] or [i for i in range(1, count) if holding[i] < most]
        pool, left = sum([portions[i] for i in free]), surplus
        for i in free:
            extra = min(most - holding[i], max(1, left * portions[i] // pool), surplus)
            holding[i] = holding[i] + extra
            surplus = surplus - extra
    return np.array(holding)


def centred(stream_key, extent, width, reach, shards=(), kind=jnp.bfloat16):
    loudness = steps_of(stream_key, extent, shards, -0.22, 0.18) if shards else 1.0
    drawn = jax.random.normal(stream_key, extent, jnp.float32) * width * loudness
    return jnp.minimum(jnp.maximum(drawn, -reach), reach).astype(kind)


def setup_inputs(seed: int = 0) -> dict:
    key_list = jax.random.split(jax.random.key(seed), 6)
    feature_maps = centred(key_list[0], (SAMPLES, SIDE, SIDE, C), 1.0, 6.0, ((0, 32),))
    path_lists_keys = jax.random.split(jax.random.fold_in(key_list[1], 1), LAYERS * SAMPLES // SMP_DEV)
    path_lists_turns = jax.random.permutation(jax.random.fold_in(key_list[1], 3), LAYERS * SAMPLES // SMP_DEV)
    path_lists = jax.vmap(lambda own, number: routed_block(jax.random.fold_in(key_list[1], 2), own, number, SMP_DEV, OPS, 1, CAP, 2))(path_lists_keys, path_lists_turns).reshape((LAYERS, SAMPLES, 1))
    point_weight = centred(key_list[2], (LAYERS, OPS, C, C), C ** -0.5, 0.1875, ((1, 2),))
    depth_kernel = centred(key_list[3], (LAYERS, OPS, TAPS, C), 0.3, 1.8, ((1, 2),), jnp.float32)
    cotangent = centred(key_list[4], (SAMPLES, SIDE, SIDE, C), 1.0, 6.0, ((0, 32),))
    return dict(feature_maps=feature_maps, path_lists=path_lists, point_weight=point_weight, depth_kernel=depth_kernel, cotangent=cotangent)


EPS = 1e-05

def tap_mask(op_kind):
    tap_index = jnp.arange(25, dtype=jnp.int32)
    row_shift = tap_index // 5 - 2
    col_shift = tap_index % 5 - 2
    narrow = (jnp.abs(row_shift) <= 1) & (jnp.abs(col_shift) <= 1)
    spaced = (row_shift % 2 == 0) & (col_shift % 2 == 0)
    tap_keep = jnp.where(op_kind == 0, narrow, jnp.where(op_kind == 1, True, spaced))
    return tap_keep.astype(jnp.float32)

def shift_window(padded, row_shift, col_shift, map_side):
    return padded[:, 2 + row_shift:2 + row_shift + map_side, 2 + col_shift:2 + col_shift + map_side, :]

def depthwise(source, kernel):
    map_side = source.shape[1]
    padded = jnp.pad(source, ((0, 0), (2, 2), (2, 2), (0, 0)))
    summed = jnp.zeros_like(source)
    for offset in range(25):
        summed = summed + kernel[offset] * shift_window(padded, offset // 5 - 2, offset % 5 - 2, map_side)
    return summed

def depthwise_back(grad_maps, kernel):
    map_side = grad_maps.shape[1]
    padded = jnp.pad(grad_maps, ((0, 0), (2, 2), (2, 2), (0, 0)))
    summed = jnp.zeros_like(grad_maps)
    for offset in range(25):
        summed = summed + kernel[offset] * shift_window(padded, 2 - offset // 5, 2 - offset % 5, map_side)
    return summed

def kernel_grad(grad_maps, source):
    map_side = source.shape[1]
    padded = jnp.pad(source, ((0, 0), (2, 2), (2, 2), (0, 0)))
    tap_rows = [lax.optimization_barrier(jnp.sum(grad_maps * shift_window(padded, offset // 5 - 2, offset % 5 - 2, map_side), axis=(0, 1, 2))) for offset in range(25)]
    return jnp.stack(tap_rows)

def block_forward(inputs, pointwise, kernel):
    channels = inputs.shape[-1]
    source = inputs.astype(jnp.float32)
    mixed_taps = depthwise(source, kernel)
    scaled = mixed_taps * lax.rsqrt(lax.optimization_barrier(jnp.mean(mixed_taps * mixed_taps, axis=-1, keepdims=True)) + EPS)
    active = (scaled * jax.nn.sigmoid(scaled)).astype(jnp.bfloat16)
    branch = jnp.dot(active.reshape(-1, channels), pointwise, preferred_element_type=jnp.float32)
    return (source + branch.reshape(source.shape)).astype(jnp.bfloat16)

def block_backward(inputs, grad_maps, pointwise, kernel):
    channels = inputs.shape[-1]
    source = inputs.astype(jnp.float32)
    mixed_taps = depthwise(source, kernel)
    inverse = lax.rsqrt(lax.optimization_barrier(jnp.mean(mixed_taps * mixed_taps, axis=-1, keepdims=True)) + EPS)
    scaled = mixed_taps * inverse
    logistic = jax.nn.sigmoid(scaled)
    active = (scaled * logistic).astype(jnp.bfloat16)
    flat_grads = grad_maps.reshape(-1, channels)
    back_act = lax.dot_general(flat_grads, pointwise, (((1,), (1,)), ((), ())), preferred_element_type=jnp.float32).reshape(source.shape)
    grad_scaled = back_act * logistic * (1.0 + scaled * (1.0 - logistic))
    grad_mixed = inverse * (grad_scaled - scaled * lax.optimization_barrier(jnp.mean(grad_scaled * scaled, axis=-1, keepdims=True)))
    grad_in = (grad_maps.astype(jnp.float32) + depthwise_back(grad_mixed, kernel)).astype(jnp.bfloat16)
    return (grad_in, active.reshape(-1, channels), flat_grads, kernel_grad(grad_mixed, source))

def point_term(active, flat_grads):
    return lax.dot_general(active, flat_grads, (((0,), (0,)), ((), ())), preferred_element_type=jnp.float32)

def reference(feature_maps, path_lists, point_weight, depth_kernel, cotangent):
    layer_inputs = []
    current = feature_maps
    for layer_at in range(LAYERS):
        layer_inputs.append(current)

        def forward_one(element):
            sample, choose = element
            kernel = depth_kernel[layer_at, choose] * tap_mask(choose % 3)[:, None]
            return block_forward(sample[None], point_weight[layer_at, choose], kernel)[0]
        current = lax.map(forward_one, (current, path_lists[layer_at, :, 0]))
    final_maps = current
    grad_maps = cotangent
    point_list = []
    depth_list = []
    for layer_at in reversed(range(LAYERS)):

        def backward_one(totals, element):
            point_acc, depth_acc = totals
            sample, grad_one, choose = element
            tap_keep = tap_mask(choose % 3)[:, None]
            kernel = depth_kernel[layer_at, choose] * tap_keep
            grad_in, active, flat_grads, depth_term = block_backward(sample[None], grad_one[None], point_weight[layer_at, choose], kernel)
            point_acc = point_acc.at[choose].add(point_term(active, flat_grads))
            depth_acc = depth_acc.at[choose].add(depth_term * tap_keep)
            return ((point_acc, depth_acc), grad_in[0])
        point_init = jnp.zeros(point_weight.shape[1:], jnp.float32)
        depth_init = jnp.zeros(depth_kernel.shape[1:], jnp.float32)
        (point_acc, depth_acc), grad_maps = lax.scan(backward_one, (point_init, depth_init), (layer_inputs[layer_at], grad_maps, path_lists[layer_at, :, 0]))
        point_list.append(point_acc)
        depth_list.append(depth_acc)
    return (final_maps, grad_maps, jnp.stack(point_list[::-1]), jnp.stack(depth_list[::-1]))
```

```python
import functools

import jax
import jax.numpy as jnp
from jax import lax
from jax.experimental import pallas as pl
from jax.experimental.pallas import tpu as pltpu
from jax.sharding import PartitionSpec as P

EPS = 1e-05
LANES = 128
F32 = jnp.float32
BF16 = jnp.bfloat16

VMEM = pl.BlockSpec(memory_space=pltpu.VMEM)
SMEM = pl.BlockSpec(memory_space=pltpu.SMEM)


def iota2(shape, axis):
    return lax.broadcasted_iota(jnp.int32, shape, axis)


def split(value, size):
    if size & (size - 1) == 0:
        return value >> (size.bit_length() - 1), value & (size - 1)
    quotient = lax.div(value, jnp.int32(size))
    return quotient, value - quotient * size


def slot_codes(path_ref, samples, capacity):
    names = [path_ref[i] for i in range(samples)]
    codes = []
    for i in range(samples):
        rank = jnp.int32(0)
        for j in range(i):
            rank = rank + jnp.where(names[j] == names[i], 1, 0)
        codes.append(names[i] * capacity + rank)
    return codes


def spread_codes(codes, which):
    out = jnp.zeros(which.shape, jnp.int32)
    for i, code in enumerate(codes):
        out = jnp.where(which == i, code, out)
    return out


def one_hot(mask):
    return jnp.where(mask, 1.0, 0.0).astype(BF16)


def pick(matrix, rows):
    return lax.dot_general(matrix, rows, (((1,), (0,)), ((), ())), preferred_element_type=F32)


def pack_kernel(path_ref, at_ref, maps_ref, *out_refs, sizes):
    places, samples, sections, capacity = sizes
    codes = slot_codes(path_ref, samples, capacity)
    shape = (places * capacity, places * samples)
    row_place, row_slot = split(iota2(shape, 0), capacity)
    col = iota2((1, places * samples), 1)
    col_place, col_sample = split(col, samples)
    col_code = spread_codes(codes, col_sample)
    for shift in range(1, sections):
        target = lax.rem(at_ref[0] + shift, sections)
        mask = (row_place == col_place) & (col_code == target * capacity + row_slot)
        out_refs[shift - 1][...] = pick(one_hot(mask), maps_ref[...]).astype(BF16)


def gather_slots(path_ref, at_ref, maps_ref, got_refs, sizes):
    places, samples, sections, capacity = sizes
    slots = sections * capacity
    codes = slot_codes(path_ref, samples, capacity)
    shape = (places * slots, places * samples)
    row_place, row_slot = split(iota2(shape, 0), slots)
    col_place, col_sample = split(iota2((1, places * samples), 1), samples)
    col_code = spread_codes(codes, col_sample)
    mask = (
        (row_place == col_place)
        & (row_slot < capacity)
        & (col_code == at_ref[0] * capacity + row_slot)
    )
    total = pick(one_hot(mask), maps_ref[...])
    shape = (places * slots, places * capacity)
    row_place, row_slot = split(iota2(shape, 0), slots)
    col_place, col_slot = split(iota2((1, places * capacity), 1), capacity)
    for shift in range(1, sections):
        mask = (row_place == col_place) & (row_slot == shift * capacity + col_slot)
        total = total + pick(one_hot(mask), got_refs[shift - 1][...])
    return total


def return_slots(slot_rows, out_refs, sizes):
    places, samples, sections, capacity = sizes
    slots = sections * capacity
    shape = (places * capacity, places * slots)
    row_place, row_slot = split(iota2(shape, 0), capacity)
    col_place, col_slot = split(iota2((1, places * slots), 1), slots)
    for shift in range(1, sections):
        mask = (row_place == col_place) & (col_slot == shift * capacity + row_slot)
        out_refs[shift - 1][...] = pick(one_hot(mask), slot_rows).astype(BF16)


def unpack_kernel(path_ref, at_ref, slots_ref, *refs, sizes):
    places, samples, sections, capacity = sizes
    slots = sections * capacity
    got_refs, out_ref = refs[:-1], refs[-1]
    codes = slot_codes(path_ref, samples, capacity)
    row = iota2((places * samples, 1), 0)
    row_place, row_sample = split(row, samples)
    row_code = spread_codes(codes, row_sample)
    col_place, col_slot = split(iota2((places * samples, places * slots), 1), slots)
    mask = (
        (row_place == col_place)
        & (col_slot < capacity)
        & (row_code == at_ref[0] * capacity + col_slot)
    )
    total = pick(one_hot(mask), slots_ref[...])
    col_place, col_slot = split(iota2((places * samples, places * capacity), 1), capacity)
    for shift in range(1, sections):
        target = lax.rem(at_ref[0] + shift, sections)
        mask = (row_place == col_place) & (row_code == target * capacity + col_slot)
        total = total + pick(one_hot(mask), got_refs[shift - 1][...])
    out_ref[...] = total.astype(BF16)


def tap_keep(kind, tap):
    row_shift, col_shift = tap // 5 - 2, tap % 5 - 2
    narrow = abs(row_shift) <= 1 and abs(col_shift) <= 1
    spaced = row_shift % 2 == 0 and col_shift % 2 == 0
    keep = kind == 1
    if narrow:
        keep = keep | (kind == 0)
    if spaced:
        keep = keep | (kind == 2)
    return jnp.where(keep, 1.0, 0.0).astype(F32)


def correlate(source_ref, kernel_ref, kind, side, slots, sign, emit):
    channels = source_ref.shape[-1]

    def chunk(at, carry):
        lanes = pl.ds(pl.multiple_of(at * LANES, LANES), LANES)
        taps = [
            jnp.broadcast_to(kernel_ref[tap, :, lanes], (slots, LANES)) * tap_keep(kind, tap)
            for tap in range(25)
        ]
        for row in range(side):
            sums = [None] * side
            for row_shift in range(-2, 3):
                source_row = row + sign * row_shift
                if not 0 <= source_row < side:
                    continue
                cells = [
                    source_ref[pl.ds((source_row * side + col) * slots, slots), lanes]
                    for col in range(side)
                ]
                for col_shift in range(-2, 3):
                    tap = taps[(row_shift + 2) * 5 + col_shift + 2]
                    for col in range(side):
                        source_col = col + sign * col_shift
                        if not 0 <= source_col < side:
                            continue
                        term = tap * cells[source_col]
                        sums[col] = term if sums[col] is None else sums[col] + term
            for col in range(side):
                emit(pl.ds((row * side + col) * slots, slots), lanes, sums[col])
        return carry

    lax.fori_loop(0, channels // LANES, chunk, 0)


def forward_kernel(path_ref, at_ref, maps_ref, weight_ref, kernel_ref, *refs, sizes, side):
    places, samples, sections, capacity = sizes
    slots = sections * capacity
    got_refs, refs = refs[: sections - 1], refs[sections - 1 :]
    back_refs, refs = refs[: sections - 1], refs[sections - 1 :]
    final_ref, active_ref, scaled_ref, inverse_ref, source_ref = refs
    kind = lax.rem(at_ref[0], 3)
    source_ref[...] = gather_slots(path_ref, at_ref, maps_ref, got_refs, sizes)

    def emit(rows, lanes, value):
        scaled_ref[rows, lanes] = value

    correlate(source_ref, kernel_ref, kind, side, slots, 1, emit)
    block = side * slots
    for row in range(side):
        rows = pl.ds(row * block, block)
        mixed = scaled_ref[rows, :]
        inverse = lax.rsqrt(jnp.mean(mixed * mixed, axis=-1, keepdims=True) + EPS)
        scaled = mixed * inverse
        scaled_ref[rows, :] = scaled
        inverse_ref[rows, :] = jnp.broadcast_to(inverse, (block, LANES))
        active_ref[rows, :] = (scaled * jax.nn.sigmoid(scaled)).astype(BF16)
    branch = pick(active_ref[...], weight_ref[...])
    final_ref[...] = (source_ref[...] + branch).astype(BF16)
    return_slots(final_ref[...], back_refs, sizes)


def point_kernel(path_ref, at_ref, grads_ref, active_ref, *refs, sizes, ways):
    places, samples, sections, capacity = sizes
    got_refs, refs = refs[: sections - 1], refs[sections - 1 :]
    slot_grads_ref, send_ref, keep_ref, total_ref = refs
    slot_grads_ref[...] = gather_slots(path_ref, at_ref, grads_ref, got_refs, sizes).astype(BF16)
    total = lax.dot_general(
        active_ref[...], slot_grads_ref[...], (((0,), (0,)), ((), ())), preferred_element_type=F32
    )
    rows = total.shape[0] // ways
    total_ref[...] = total.reshape(ways, rows, total.shape[1])
    low = at_ref[1] & 1
    for at in range(ways // 2):
        send_ref[at] = total_ref[2 * at + 1 - low].astype(BF16)
        keep_ref[at] = total_ref[2 * at + low]


def fold_kernel(at_ref, keep_ref, got_ref, send_ref, left_ref, *, stride, bit):
    count = keep_ref.shape[0]
    mine = (at_ref[1] // bit) & 1
    at = 0
    for base in range(0, count, 2 * stride):
        for offset in range(stride):
            give = base + offset + stride * (1 - mine)
            hold = base + offset + stride * mine
            send_ref[at] = (keep_ref[give] + got_ref[give].astype(F32)).astype(BF16)
            left_ref[at] = keep_ref[hold] + got_ref[hold].astype(F32)
            at += 1


def last_kernel(keep_a_ref, got_a_ref, keep_b_ref, got_b_ref, out_ref):
    half = keep_a_ref.shape[-1]
    out_ref[:, :half] = keep_a_ref[0] + got_a_ref[0].astype(F32)
    out_ref[:, half:] = keep_b_ref[0] + got_b_ref[0].astype(F32)


def backward_kernel(
    at_ref, slot_grads_ref, weight_ref, kernel_ref, scaled_ref, inverse_ref, *refs, sizes, side
):
    places, samples, sections, capacity = sizes
    slots = sections * capacity
    back_refs, refs = refs[: sections - 1], refs[sections - 1 :]
    grad_in_ref, mixed_ref, work_ref = refs
    kind = lax.rem(at_ref[0], 3)
    work_ref[...] = lax.dot_general(
        slot_grads_ref[...], weight_ref[...], (((1,), (1,)), ((), ())), preferred_element_type=F32
    )
    block = side * slots
    for row in range(side):
        rows = pl.ds(row * block, block)
        scaled = scaled_ref[rows, :]
        logistic = jax.nn.sigmoid(scaled)
        grad_scaled = work_ref[rows, :] * logistic * (1.0 + scaled * (1.0 - logistic))
        mean = jnp.mean(grad_scaled * scaled, axis=-1, keepdims=True)
        mixed_ref[rows, :] = inverse_ref[rows, :1] * (grad_scaled - scaled * mean)

    def emit(rows, lanes, value):
        work_ref[rows, lanes] = value

    correlate(mixed_ref, kernel_ref, kind, side, slots, -1, emit)
    grad_in_ref[...] = (slot_grads_ref[...].astype(F32) + work_ref[...]).astype(BF16)
    return_slots(grad_in_ref[...], back_refs, sizes)


def taps_kernel(at_ref, mixed_ref, source_ref, out_ref, *, side, slots):
    kind = lax.rem(at_ref[0], 3)
    channels = mixed_ref.shape[-1]

    def chunk(at, carry):
        lanes = pl.ds(pl.multiple_of(at * LANES, LANES), LANES)

        def cells(ref, row):
            return [ref[pl.ds((row * side + col) * slots, slots), lanes] for col in range(side)]

        sums = [None] * 25
        for row in range(side):
            grads = cells(mixed_ref, row)
            for row_shift in range(-2, 3):
                if not 0 <= row + row_shift < side:
                    continue
                source = cells(source_ref, row + row_shift)
                for col_shift in range(-2, 3):
                    tap = (row_shift + 2) * 5 + col_shift + 2
                    for col in range(side):
                        if not 0 <= col + col_shift < side:
                            continue
                        term = grads[col] * source[col + col_shift]
                        sums[tap] = term if sums[tap] is None else sums[tap] + term
        for tap in range(25):
            out_ref[tap, :, lanes] = (
                jnp.sum(sums[tap], axis=0, keepdims=True) * tap_keep(kind, tap)
            )
        return carry

    lax.fori_loop(0, channels // LANES, chunk, 0)


def call(kernel, name, outs, in_specs, scratch=()):
    return pl.pallas_call(
        kernel,
        out_shape=outs,
        in_specs=in_specs,
        out_specs=jax.tree.map(lambda _: VMEM, outs),
        scratch_shapes=list(scratch),
        compiler_params=pltpu.CompilerParams(vmem_limit_bytes=56 * 1024 * 1024),
        name=name,
    )


def body(feature_maps, path_lists, point_weight, depth_kernel, cotangent):
    sections = lax.axis_size("segment")
    ways = lax.axis_size("rep")
    section = lax.axis_index("segment").astype(jnp.int32)
    replica = lax.axis_index("rep").astype(jnp.int32)
    samples, side, _, channels = feature_maps.shape
    places = side * side
    capacity = max(max(2, samples // 4), (samples + sections - 1) // sections)
    slots = sections * capacity
    sizes = (places, samples, sections, capacity)
    at = jnp.stack([section, replica])
    path = path_lists[0, :, 0]
    weight = point_weight[0, 0]
    kernel = depth_kernel[0, 0].reshape(25, 1, channels)
    others = range(1, sections)

    def rows_of(maps):
        return jnp.transpose(maps, (1, 2, 0, 3)).reshape(places * samples, channels)

    def maps_of(rows):
        return jnp.transpose(rows.reshape(side, side, samples, channels), (2, 0, 1, 3))

    def shape(*dims, dtype=F32):
        return jax.ShapeDtypeStruct(dims, dtype)

    packed = shape(places * capacity, channels, dtype=BF16)

    def pack(rows):
        return call(
            functools.partial(pack_kernel, sizes=sizes),
            "pack",
            [packed for _ in others],
            [SMEM, SMEM, VMEM],
        )(path, at, rows)

    def swap(pieces, direction):
        return [
            lax.ppermute(
                piece,
                "segment",
                [(i, (i + direction * shift) % sections) for i in range(sections)],
            )
            for shift, piece in zip(others, pieces)
        ]

    def unpack(slot_rows, pieces):
        return call(
            functools.partial(unpack_kernel, sizes=sizes),
            "unpack",
            shape(places * samples, channels, dtype=BF16),
            [SMEM, SMEM, VMEM] + [VMEM for _ in others],
        )(path, at, slot_rows, *pieces)

    def trade(value, bit):
        return lax.ppermute(value, "rep", [(i, i ^ bit) for i in range(ways)])

    maps, grads = rows_of(feature_maps), rows_of(cotangent)
    got_maps = swap(pack(maps), 1)
    got_grads = swap(pack(grads), 1)

    slot_shape = shape(places * slots, channels)
    slot_half = shape(places * slots, channels, dtype=BF16)
    results = call(
        functools.partial(forward_kernel, sizes=sizes, side=side),
        "forward",
        [packed for _ in others]
        + [slot_half, slot_half, slot_shape, shape(places * slots, LANES), slot_shape],
        [SMEM, SMEM, VMEM, VMEM, VMEM] + [VMEM for _ in others],
    )(path, at, maps, weight, kernel, *got_maps)
    back = results[: sections - 1]
    slot_final, active, scaled, inverse, source = results[sections - 1 :]
    got_final = swap(back, -1)

    block = channels // ways
    slot_grads, send, keep = call(
        functools.partial(point_kernel, sizes=sizes, ways=ways),
        "point",
        [slot_half, shape(ways // 2, block, channels, dtype=BF16), shape(ways // 2, block, channels)],
        [SMEM, SMEM, VMEM, VMEM] + [VMEM for _ in others],
        [pltpu.VMEM((ways, block, channels), F32)],
    )(path, at, grads, active, *got_grads)

    got = trade(send, 1)

    results = call(
        functools.partial(backward_kernel, sizes=sizes, side=side),
        "backward",
        [packed for _ in others] + [slot_half, slot_shape],
        [SMEM, VMEM, VMEM, VMEM, VMEM, VMEM],
        [pltpu.VMEM((places * slots, channels), F32)],
    )(at, slot_grads, weight, kernel, scaled, inverse)
    back = results[: sections - 1]
    slot_in, mixed = results[sections - 1 :]
    got_in = swap(back, -1)

    taps = call(
        functools.partial(taps_kernel, side=side, slots=slots),
        "taps",
        shape(25, 1, channels),
        [SMEM, VMEM, VMEM],
    )(at, mixed, source)

    bits = [1 << i for i in range(1, ways.bit_length() - 1)]
    half = channels // 2
    finished = []
    for part in range(2):
        order = list(bits)
        if part == 1 and len(order) > 1:
            order[0], order[1] = order[1], order[0]
        left = list(bits)
        columns = slice(part * half, (part + 1) * half)
        keep_part, got_part = keep[:, :, columns], got[:, :, columns]
        for bit in order:
            stride = 1
            for other in left:
                if other < bit:
                    stride *= 2
            left.remove(bit)
            count = keep_part.shape[0] // 2
            send_part, keep_part = call(
                functools.partial(fold_kernel, stride=stride, bit=bit),
                "fold",
                [shape(count, block, half, dtype=BF16), shape(count, block, half)],
                [SMEM, VMEM, VMEM],
            )(at, keep_part, got_part)
            got_part = trade(send_part, bit)
        finished += [keep_part, got_part]
    point_grad = call(
        last_kernel, "last", shape(block, channels), [VMEM, VMEM, VMEM, VMEM]
    )(*finished)

    for bit in [1] + bits:
        taps = taps + trade(taps, bit)

    final_maps = maps_of(unpack(slot_final, got_final))
    input_grad = maps_of(unpack(slot_in, got_in))
    return (
        final_maps,
        input_grad,
        point_grad.reshape(1, 1, block, channels),
        taps.reshape(1, 1, 25, channels),
    )


def solution(mesh):
    placed = (
        P(("segment", "rep"), None, None, None),
        P(None, ("segment", "rep"), None),
        P(None, "segment", None, None),
        P(None, "segment", None, None),
        P(("segment", "rep"), None, None, None),
    )
    return jax.shard_map(
        body,
        mesh=mesh,
        in_specs=placed,
        out_specs=(
            P(("segment", "rep"), None, None, None),
            P(("segment", "rep"), None, None, None),
            P(None, "segment", "rep", None),
            P(None, "segment", None, None),
        ),
        check_vma=False,
    )
```

```python
import functools

import jax
import jax.numpy as jnp
from jax import lax
from jax.experimental import pallas as pl
from jax.experimental.pallas import tpu as pltpu
from jax.sharding import PartitionSpec as P

EPS = 1e-05
LANES = 128
F32 = jnp.float32
BF16 = jnp.bfloat16

VMEM = pl.BlockSpec(memory_space=pltpu.VMEM)
SMEM = pl.BlockSpec(memory_space=pltpu.SMEM)


def iota2(shape, axis):
    return lax.broadcasted_iota(jnp.int32, shape, axis)


def split(value, size):
    if size & (size - 1) == 0:
        return value >> (size.bit_length() - 1), value & (size - 1)
    quotient = lax.div(value, jnp.int32(size))
    return quotient, value - quotient * size


def slot_codes(path_ref, samples, capacity):
    names = [path_ref[i] for i in range(samples)]
    codes = []
    for i in range(samples):
        rank = jnp.int32(0)
        for j in range(i):
            rank = rank + jnp.where(names[j] == names[i], 1, 0)
        codes.append(names[i] * capacity + rank)
    return codes


def spread_codes(codes, which):
    out = jnp.zeros(which.shape, jnp.int32)
    for i, code in enumerate(codes):
        out = jnp.where(which == i, code, out)
    return out


def one_hot(mask):
    return jnp.where(mask, 1.0, 0.0).astype(BF16)


def pick(matrix, rows):
    return lax.dot_general(matrix, rows, (((1,), (0,)), ((), ())), preferred_element_type=F32)


def pack_kernel(path_ref, at_ref, maps_ref, *out_refs, sizes):
    places, samples, sections, capacity = sizes
    codes = slot_codes(path_ref, samples, capacity)
    shape = (places * capacity, places * samples)
    row_place, row_slot = split(iota2(shape, 0), capacity)
    col = iota2((1, places * samples), 1)
    col_place, col_sample = split(col, samples)
    col_code = spread_codes(codes, col_sample)
    for shift in range(1, sections):
        target = lax.rem(at_ref[0] + shift, sections)
        mask = (row_place == col_place) & (col_code == target * capacity + row_slot)
        out_refs[shift - 1][...] = pick(one_hot(mask), maps_ref[...]).astype(BF16)


def gather_slots(path_ref, at_ref, maps_ref, got_refs, sizes):
    places, samples, sections, capacity = sizes
    slots = sections * capacity
    codes = slot_codes(path_ref, samples, capacity)
    shape = (places * slots, places * samples)
    row_place, row_slot = split(iota2(shape, 0), slots)
    col_place, col_sample = split(iota2((1, places * samples), 1), samples)
    col_code = spread_codes(codes, col_sample)
    mask = (
        (row_place == col_place)
        & (row_slot < capacity)
        & (col_code == at_ref[0] * capacity + row_slot)
    )
    total = pick(one_hot(mask), maps_ref[...])
    shape = (places * slots, places * capacity)
    row_place, row_slot = split(iota2(shape, 0), slots)
    col_place, col_slot = split(iota2((1, places * capacity), 1), capacity)
    for shift in range(1, sections):
        mask = (row_place == col_place) & (row_slot == shift * capacity + col_slot)
        total = total + pick(one_hot(mask), got_refs[shift - 1][...])
    return total


def return_slots(slot_rows, out_refs, sizes):
    places, samples, sections, capacity = sizes
    slots = sections * capacity
    shape = (places * capacity, places * slots)
    row_place, row_slot = split(iota2(shape, 0), capacity)
    col_place, col_slot = split(iota2((1, places * slots), 1), slots)
    for shift in range(1, sections):
        mask = (row_place == col_place) & (col_slot == shift * capacity + row_slot)
        out_refs[shift - 1][...] = pick(one_hot(mask), slot_rows).astype(BF16)


def unpack_kernel(path_ref, at_ref, slots_ref, *refs, sizes):
    places, samples, sections, capacity = sizes
    slots = sections * capacity
    got_refs, out_ref = refs[:-1], refs[-1]
    codes = slot_codes(path_ref, samples, capacity)
    row = iota2((places * samples, 1), 0)
    row_place, row_sample = split(row, samples)
    row_code = spread_codes(codes, row_sample)
    col_place, col_slot = split(iota2((places * samples, places * slots), 1), slots)
    mask = (
        (row_place == col_place)
        & (col_slot < capacity)
        & (row_code == at_ref[0] * capacity + col_slot)
    )
    total = pick(one_hot(mask), slots_ref[...])
    col_place, col_slot = split(iota2((places * samples, places * capacity), 1), capacity)
    for shift in range(1, sections):
        target = lax.rem(at_ref[0] + shift, sections)
        mask = (row_place == col_place) & (row_code == target * capacity + col_slot)
        total = total + pick(one_hot(mask), got_refs[shift - 1][...])
    out_ref[...] = total.astype(BF16)


def tap_keep(kind, tap):
    row_shift, col_shift = tap // 5 - 2, tap % 5 - 2
    narrow = abs(row_shift) <= 1 and abs(col_shift) <= 1
    spaced = row_shift % 2 == 0 and col_shift % 2 == 0
    keep = kind == 1
    if narrow:
        keep = keep | (kind == 0)
    if spaced:
        keep = keep | (kind == 2)
    return jnp.where(keep, 1.0, 0.0).astype(F32)


def correlate(source_ref, kernel_ref, kind, side, slots, sign, emit):
    channels = source_ref.shape[-1]

    def chunk(at, carry):
        lanes = pl.ds(pl.multiple_of(at * LANES, LANES), LANES)
        taps = [
            jnp.broadcast_to(kernel_ref[tap, :, lanes], (slots, LANES)) * tap_keep(kind, tap)
            for tap in range(25)
        ]
        for row in range(side):
            sums = [None] * side
            for row_shift in range(-2, 3):
                source_row = row + sign * row_shift
                if not 0 <= source_row < side:
                    continue
                cells = [
                    source_ref[pl.ds((source_row * side + col) * slots, slots), lanes]
                    for col in range(side)
                ]
                for col_shift in range(-2, 3):
                    tap = taps[(row_shift + 2) * 5 + col_shift + 2]
                    for col in range(side):
                        source_col = col + sign * col_shift
                        if not 0 <= source_col < side:
                            continue
                        term = tap * cells[source_col]
                        sums[col] = term if sums[col] is None else sums[col] + term
            for col in range(side):
                emit(pl.ds((row * side + col) * slots, slots), lanes, sums[col])
        return carry

    lax.fori_loop(0, channels // LANES, chunk, 0)


def forward_kernel(path_ref, at_ref, maps_ref, weight_ref, kernel_ref, *refs, sizes, side):
    places, samples, sections, capacity = sizes
    slots = sections * capacity
    got_refs, refs = refs[: sections - 1], refs[sections - 1 :]
    back_refs, refs = refs[: sections - 1], refs[sections - 1 :]
    final_ref, active_ref, scaled_ref, inverse_ref, source_ref = refs
    kind = lax.rem(at_ref[0], 3)
    source_ref[...] = gather_slots(path_ref, at_ref, maps_ref, got_refs, sizes)

    def emit(rows, lanes, value):
        scaled_ref[rows, lanes] = value

    correlate(source_ref, kernel_ref, kind, side, slots, 1, emit)
    block = side * slots
    for row in range(side):
        rows = pl.ds(row * block, block)
        mixed = scaled_ref[rows, :]
        inverse = lax.rsqrt(jnp.mean(mixed * mixed, axis=-1, keepdims=True) + EPS)
        scaled = mixed * inverse
        scaled_ref[rows, :] = scaled
        inverse_ref[rows, :] = jnp.broadcast_to(inverse, (block, LANES))
        active_ref[rows, :] = (scaled * jax.nn.sigmoid(scaled)).astype(BF16)
    branch = pick(active_ref[...], weight_ref[...])
    final_ref[...] = (source_ref[...] + branch).astype(BF16)
    return_slots(final_ref[...], back_refs, sizes)


def point_kernel(path_ref, at_ref, replica_ref, grads_ref, active_ref, *refs, sizes, ways):
    places, samples, sections, capacity = sizes
    got_refs, refs = refs[: sections - 1], refs[sections - 1 :]
    slot_grads_ref, send_ref, keep_ref, total_ref = refs
    slot_grads_ref[...] = gather_slots(path_ref, at_ref, grads_ref, got_refs, sizes).astype(BF16)
    total = lax.dot_general(
        active_ref[...], slot_grads_ref[...], (((0,), (0,)), ((), ())), preferred_element_type=F32
    )
    rows = total.shape[0] // ways
    total_ref[...] = total.reshape(ways, rows, total.shape[1])
    low = replica_ref[0] & 1
    for at in range(ways // 2):
        send_ref[at] = total_ref[2 * at + 1 - low].astype(BF16)
        keep_ref[at] = total_ref[2 * at + low]


def fold_kernel(replica_ref, *refs, moves, arriving):
    ins, outs = refs[:arriving], refs[arriving:]
    for (stride, bit), (source, came), (target, goes) in moves:
        keep_ref, got_ref = ins[2 * source], ins[2 * source + 1]
        send_ref, left_ref = outs[2 * target], outs[2 * target + 1]
        count = keep_ref.shape[0]
        mine = (replica_ref[0] // bit) & 1
        at = 0
        for base in range(0, count, 2 * stride):
            for offset in range(stride):
                give = base + offset + stride * (1 - mine)
                hold = base + offset + stride * mine
                send_ref[at, :, goes] = (
                    keep_ref[give, :, came] + got_ref[give, :, came].astype(F32)
                ).astype(BF16)
                left_ref[at, :, goes] = keep_ref[hold, :, came] + got_ref[hold, :, came].astype(F32)
                at += 1


def backward_kernel(
    at_ref, slot_grads_ref, weight_ref, kernel_ref, scaled_ref, inverse_ref, *refs, sizes, side
):
    places, samples, sections, capacity = sizes
    slots = sections * capacity
    back_refs, refs = refs[: sections - 1], refs[sections - 1 :]
    grad_in_ref, mixed_ref, work_ref = refs
    kind = lax.rem(at_ref[0], 3)
    work_ref[...] = lax.dot_general(
        slot_grads_ref[...], weight_ref[...], (((1,), (1,)), ((), ())), preferred_element_type=F32
    )
    block = side * slots
    for row in range(side):
        rows = pl.ds(row * block, block)
        scaled = scaled_ref[rows, :]
        logistic = jax.nn.sigmoid(scaled)
        grad_scaled = work_ref[rows, :] * logistic * (1.0 + scaled * (1.0 - logistic))
        mean = jnp.mean(grad_scaled * scaled, axis=-1, keepdims=True)
        mixed_ref[rows, :] = inverse_ref[rows, :1] * (grad_scaled - scaled * mean)

    def emit(rows, lanes, value):
        work_ref[rows, lanes] = value

    correlate(mixed_ref, kernel_ref, kind, side, slots, -1, emit)
    grad_in_ref[...] = (slot_grads_ref[...].astype(F32) + work_ref[...]).astype(BF16)
    return_slots(grad_in_ref[...], back_refs, sizes)


def taps_kernel(at_ref, mixed_ref, source_ref, out_ref, *, side, slots):
    kind = lax.rem(at_ref[0], 3)
    channels = mixed_ref.shape[-1]

    def chunk(at, carry):
        lanes = pl.ds(pl.multiple_of(at * LANES, LANES), LANES)

        def cells(ref, row):
            return [ref[pl.ds((row * side + col) * slots, slots), lanes] for col in range(side)]

        sums = [None] * 25
        for row in range(side):
            grads = cells(mixed_ref, row)
            for row_shift in range(-2, 3):
                if not 0 <= row + row_shift < side:
                    continue
                source = cells(source_ref, row + row_shift)
                for col_shift in range(-2, 3):
                    tap = (row_shift + 2) * 5 + col_shift + 2
                    for col in range(side):
                        if not 0 <= col + col_shift < side:
                            continue
                        term = grads[col] * source[col + col_shift]
                        sums[tap] = term if sums[tap] is None else sums[tap] + term
        for tap in range(25):
            out_ref[tap, :, lanes] = (
                jnp.sum(sums[tap], axis=0, keepdims=True) * tap_keep(kind, tap)
            )
        return carry

    lax.fori_loop(0, channels // LANES, chunk, 0)


def call(kernel, name, outs, in_specs, scratch=(), megabytes=20):
    return pl.pallas_call(
        kernel,
        out_shape=outs,
        in_specs=in_specs,
        out_specs=jax.tree.map(lambda _: VMEM, outs),
        scratch_shapes=list(scratch),
        compiler_params=pltpu.CompilerParams(vmem_limit_bytes=megabytes * 1024 * 1024),
        name=name,
    )


def body(feature_maps, path_lists, point_weight, depth_kernel, cotangent):
    sections = lax.axis_size("segment")
    ways = lax.axis_size("rep")
    at = lax.axis_index("segment").astype(jnp.int32).reshape(1)
    replica = lax.axis_index("rep").astype(jnp.int32).reshape(1)
    samples, side, _, channels = feature_maps.shape
    places = side * side
    capacity = max(max(2, samples // 4), (samples + sections - 1) // sections)
    slots = sections * capacity
    sizes = (places, samples, sections, capacity)
    path = path_lists[0, :, 0]
    weight = point_weight[0, 0]
    kernel = depth_kernel[0, 0].reshape(25, 1, channels)
    others = range(1, sections)

    def rows_of(maps):
        return jnp.transpose(maps, (1, 2, 0, 3)).reshape(places * samples, channels)

    def maps_of(rows):
        return jnp.transpose(rows.reshape(side, side, samples, channels), (2, 0, 1, 3))

    def shape(*dims, dtype=F32):
        return jax.ShapeDtypeStruct(dims, dtype)

    packed = shape(places * capacity, channels, dtype=BF16)

    def pack(rows):
        return call(
            functools.partial(pack_kernel, sizes=sizes),
            "pack",
            [packed for _ in others],
            [SMEM, SMEM, VMEM],
        )(path, at, rows)

    def swap(pieces, direction):
        return [
            lax.ppermute(
                piece,
                "segment",
                [(i, (i + direction * shift) % sections) for i in range(sections)],
            )
            for shift, piece in zip(others, pieces)
        ]

    def unpack(slot_rows, pieces):
        return call(
            functools.partial(unpack_kernel, sizes=sizes),
            "unpack",
            shape(places * samples, channels, dtype=BF16),
            [SMEM, SMEM, VMEM] + [VMEM for _ in others],
        )(path, at, slot_rows, *pieces)

    def trade(value, bit):
        return lax.ppermute(value, "rep", [(i, i ^ bit) for i in range(ways)])

    maps, grads = rows_of(feature_maps), rows_of(cotangent)
    got_maps = swap(pack(maps), 1)
    got_grads = swap(pack(grads), 1)

    slot_shape = shape(places * slots, channels)
    slot_half = shape(places * slots, channels, dtype=BF16)
    results = call(
        functools.partial(forward_kernel, sizes=sizes, side=side),
        "forward",
        [packed for _ in others]
        + [slot_half, slot_half, slot_shape, shape(places * slots, LANES), slot_shape],
        [SMEM, SMEM, VMEM, VMEM, VMEM] + [VMEM for _ in others],
    )(path, at, maps, weight, kernel, *got_maps)
    back = results[: sections - 1]
    slot_final, active, scaled, inverse, source = results[sections - 1 :]
    got_final = swap(back, -1)

    block = channels // ways
    slot_grads, send, keep = call(
        functools.partial(point_kernel, sizes=sizes, ways=ways),
        "point",
        [slot_half, shape(ways // 2, block, channels, dtype=BF16), shape(ways // 2, block, channels)],
        [SMEM, SMEM, SMEM, VMEM, VMEM] + [VMEM for _ in others],
        [pltpu.VMEM((ways, block, channels), F32)],
    )(path, at, replica, grads, active, *got_grads)

    got = trade(send, 1)

    results = call(
        functools.partial(backward_kernel, sizes=sizes, side=side),
        "backward",
        [packed for _ in others] + [slot_half, slot_shape],
        [SMEM, VMEM, VMEM, VMEM, VMEM, VMEM],
        [pltpu.VMEM((places * slots, channels), F32)],
    )(at, slot_grads, weight, kernel, scaled, inverse)
    back = results[: sections - 1]
    slot_in, mixed = results[sections - 1 :]
    got_in = swap(back, -1)

    taps = call(
        functools.partial(taps_kernel, side=side, slots=slots),
        "taps",
        shape(25, 1, channels),
        [SMEM, VMEM, VMEM],
    )(at, mixed, source)

    bits = [1 << i for i in range(1, ways.bit_length() - 1)]
    orders = [list(bits), list(bits)]
    if len(bits) > 2:
        orders[1][0], orders[1][1] = bits[1], bits[0]
    half = channels // 2
    halves = [slice(0, half), slice(half, channels)]
    held = [keep, got]
    for step in range(len(bits)):
        first, final = step == 0, step == len(bits) - 1
        count = (ways // 4) >> step
        moves = []
        for part in range(2):
            bit = orders[part][step]
            done = orders[part][:step]
            stride = 1 << sum(1 for other in bits if other < bit and other not in done)
            moves.append(
                (
                    (stride, bit),
                    (0, halves[part]) if first else (part, slice(0, half)),
                    (0, halves[part]) if final else (part, slice(0, half)),
                )
            )
        width, targets = (channels, 1) if final else (half, 2)
        outs = [shape(count, block, width, dtype=BF16), shape(count, block, width)] * targets
        results = call(
            functools.partial(fold_kernel, moves=moves, arriving=len(held)),
            "fold",
            outs,
            [SMEM] + [VMEM] * len(held),
        )(replica, *held)
        held = []
        for part in range(targets):
            held += [results[2 * part + 1], trade(results[2 * part], orders[part][step])]
    point_grad = (held[0] + held[1].astype(F32))[0]

    for bit in [1] + bits:
        taps = taps + trade(taps, bit)

    final_maps = maps_of(unpack(slot_final, got_final))
    input_grad = maps_of(unpack(slot_in, got_in))
    return (
        final_maps,
        input_grad,
        point_grad.reshape(1, 1, block, channels),
        taps.reshape(1, 1, 25, channels),
    )


def solution(mesh):
    placed = (
        P(("segment", "rep"), None, None, None),
        P(None, ("segment", "rep"), None),
        P(None, "segment", None, None),
        P(None, "segment", None, None),
        P(("segment", "rep"), None, None, None),
    )
    return jax.shard_map(
        body,
        mesh=mesh,
        in_specs=placed,
        out_specs=(
            P(("segment", "rep"), None, None, None),
            P(("segment", "rep"), None, None, None),
            P(None, "segment", "rep", None),
            P(None, "segment", None, None),
        ),
        check_vma=False,
    )
```

```python
import functools

import jax
import jax.numpy as jnp
from jax import lax
from jax.experimental import pallas as pl
from jax.experimental.pallas import tpu as pltpu
from jax.sharding import PartitionSpec as P


EPS = 1e-05
LANES = 128
F32 = jnp.float32
BF16 = jnp.bfloat16

VMEM = pl.BlockSpec(memory_space=pltpu.VMEM)
SMEM = pl.BlockSpec(memory_space=pltpu.SMEM)


def iota2(shape, axis):
    return lax.broadcasted_iota(jnp.int32, shape, axis)


def split(value, size):
    if size & (size - 1) == 0:
        return value >> (size.bit_length() - 1), value & (size - 1)
    quotient = lax.div(value, jnp.int32(size))
    return quotient, value - quotient * size


def slot_codes(path_ref, samples, capacity):
    names = [path_ref[i] for i in range(samples)]
    codes = []
    for i in range(samples):
        rank = jnp.int32(0)
        for j in range(i):
            rank = rank + jnp.where(names[j] == names[i], 1, 0)
        codes.append(names[i] * capacity + rank)
    return codes


def spread_codes(codes, which):
    out = jnp.zeros(which.shape, jnp.int32)
    for i, code in enumerate(codes):
        out = jnp.where(which == i, code, out)
    return out


def one_hot(mask):
    return jnp.where(mask, 1.0, 0.0).astype(BF16)


def pick(matrix, rows):
    return lax.dot_general(matrix, rows, (((1,), (0,)), ((), ())), preferred_element_type=F32)


def pack_kernel(path_ref, at_ref, maps_ref, *out_refs, sizes):
    places, samples, sections, capacity = sizes
    codes = slot_codes(path_ref, samples, capacity)
    shape = (places * capacity, places * samples)
    row_place, row_slot = split(iota2(shape, 0), capacity)
    col = iota2((1, places * samples), 1)
    col_place, col_sample = split(col, samples)
    col_code = spread_codes(codes, col_sample)
    for shift in range(1, sections):
        target = lax.rem(at_ref[0] + shift, sections)
        mask = (row_place == col_place) & (col_code == target * capacity + row_slot)
        out_refs[shift - 1][...] = pick(one_hot(mask), maps_ref[...]).astype(BF16)


def prepare_kernel(
    path_ref, at_ref, maps_ref, grads_ref, kernel_ref, own_maps_ref, own_grads_ref, taps_ref, *, sizes
):
    places, samples, sections, capacity = sizes
    slots = sections * capacity
    codes = slot_codes(path_ref, samples, capacity)
    row_place, row_slot = split(iota2((places * slots, places * samples), 0), slots)
    col_place, col_sample = split(iota2((1, places * samples), 1), samples)
    col_code = spread_codes(codes, col_sample)
    mask = (
        (row_place == col_place)
        & (row_slot < capacity)
        & (col_code == at_ref[0] * capacity + row_slot)
    )
    matrix = one_hot(mask)
    own_maps_ref[...] = pick(matrix, maps_ref[...]).astype(BF16)
    own_grads_ref[...] = pick(matrix, grads_ref[...]).astype(BF16)
    kind = lax.rem(at_ref[0], 3)
    for tap in range(25):
        taps_ref[tap] = kernel_ref[tap] * tap_keep(kind, tap)


def gather_slots(own_ref, got_refs, sizes):
    places, _, sections, capacity = sizes
    slots = sections * capacity
    total = own_ref[...].astype(F32)
    row_place, row_slot = split(iota2((places * slots, places * capacity), 0), slots)
    col_place, col_slot = split(iota2((1, places * capacity), 1), capacity)
    for shift in range(1, sections):
        mask = (row_place == col_place) & (row_slot == shift * capacity + col_slot)
        total = total + pick(one_hot(mask), got_refs[shift - 1][...])
    return total


def return_slots(slot_rows, out_refs, sizes):
    places, _, sections, capacity = sizes
    slots = sections * capacity
    shape = (places * capacity, places * slots)
    row_place, row_slot = split(iota2(shape, 0), capacity)
    col_place, col_slot = split(iota2((1, places * slots), 1), slots)
    for shift in range(1, sections):
        mask = (row_place == col_place) & (col_slot == shift * capacity + row_slot)
        out_refs[shift - 1][...] = pick(one_hot(mask), slot_rows).astype(BF16)


def unpack_kernel(path_ref, at_ref, slots_ref, *refs, sizes):
    places, samples, sections, capacity = sizes
    slots = sections * capacity
    got_refs, out_ref = refs[:-1], refs[-1]
    codes = slot_codes(path_ref, samples, capacity)
    row = iota2((places * samples, 1), 0)
    row_place, row_sample = split(row, samples)
    row_code = spread_codes(codes, row_sample)
    col_place, col_slot = split(iota2((places * samples, places * slots), 1), slots)
    mask = (
        (row_place == col_place)
        & (col_slot < capacity)
        & (row_code == at_ref[0] * capacity + col_slot)
    )
    total = pick(one_hot(mask), slots_ref[...])
    col_place, col_slot = split(iota2((places * samples, places * capacity), 1), capacity)
    for shift in range(1, sections):
        target = lax.rem(at_ref[0] + shift, sections)
        mask = (row_place == col_place) & (row_code == target * capacity + col_slot)
        total = total + pick(one_hot(mask), got_refs[shift - 1][...])
    out_ref[...] = total.astype(BF16)


def tap_keep(kind, tap):
    row_shift, col_shift = tap // 5 - 2, tap % 5 - 2
    narrow = abs(row_shift) <= 1 and abs(col_shift) <= 1
    spaced = row_shift % 2 == 0 and col_shift % 2 == 0
    keep = kind == 1
    if narrow:
        keep = keep | (kind == 0)
    if spaced:
        keep = keep | (kind == 2)
    return jnp.where(keep, 1.0, 0.0).astype(F32)


def correlate(source_ref, kernel_ref, side, slots, sign, emit):
    channels = source_ref.shape[-1]

    def chunk(at, carry):
        lanes = pl.ds(pl.multiple_of(at * LANES, LANES), LANES)
        taps = [
            jnp.broadcast_to(kernel_ref[tap, :, lanes], (slots, LANES)) for tap in range(25)
        ]
        for row in range(side):
            sums = [None] * side
            for row_shift in range(-2, 3):
                source_row = row + sign * row_shift
                if not 0 <= source_row < side:
                    continue
                cells = [
                    source_ref[pl.ds((source_row * side + col) * slots, slots), lanes]
                    for col in range(side)
                ]
                for col_shift in range(-2, 3):
                    tap = taps[(row_shift + 2) * 5 + col_shift + 2]
                    for col in range(side):
                        source_col = col + sign * col_shift
                        if not 0 <= source_col < side:
                            continue
                        term = tap * cells[source_col]
                        sums[col] = term if sums[col] is None else sums[col] + term
            for col in range(side):
                emit(pl.ds((row * side + col) * slots, slots), lanes, sums[col])
        return carry

    lax.fori_loop(0, channels // LANES, chunk, 0)


def forward_kernel(own_ref, weight_ref, kernel_ref, *refs, sizes, side):
    _, _, sections, capacity = sizes
    slots = sections * capacity
    got_refs, refs = refs[: sections - 1], refs[sections - 1 :]
    back_refs, refs = refs[: sections - 1], refs[sections - 1 :]
    final_ref, active_ref, scaled_ref, inverse_ref, source_ref = refs
    source_ref[...] = gather_slots(own_ref, got_refs, sizes)

    def emit(rows, lanes, value):
        scaled_ref[rows, lanes] = value

    correlate(source_ref, kernel_ref, side, slots, 1, emit)
    block = side * slots
    for row in range(side):
        rows = pl.ds(row * block, block)
        mixed = scaled_ref[rows, :]
        inverse = lax.rsqrt(jnp.mean(mixed * mixed, axis=-1, keepdims=True) + EPS)
        scaled = mixed * inverse
        scaled_ref[rows, :] = scaled
        inverse_ref[rows, :] = jnp.broadcast_to(inverse, (block, LANES))
        active_ref[rows, :] = (scaled * jax.nn.sigmoid(scaled)).astype(BF16)
    branch = pick(active_ref[...], weight_ref[...])
    final_ref[...] = (source_ref[...] + branch).astype(BF16)
    return_slots(final_ref[...], back_refs, sizes)


def point_kernel(replica_ref, own_ref, active_ref, *refs, sizes, ways):
    _, _, sections, _ = sizes
    got_refs, refs = refs[: sections - 1], refs[sections - 1 :]
    slot_grads_ref, send_ref, keep_ref, total_ref = refs
    slot_grads_ref[...] = gather_slots(own_ref, got_refs, sizes).astype(BF16)
    total = lax.dot_general(
        active_ref[...], slot_grads_ref[...], (((0,), (0,)), ((), ())), preferred_element_type=F32
    )
    rows = total.shape[0] // ways
    total_ref[...] = total.reshape(ways, rows, total.shape[1])
    low = replica_ref[0] & 1
    for at in range(ways // 2):
        send_ref[at] = total_ref[2 * at + 1 - low].astype(BF16)
        keep_ref[at] = total_ref[2 * at + low]


def fold_kernel(replica_ref, *refs, moves, arriving):
    ins, outs = refs[:arriving], refs[arriving:]
    for (stride, bit), (source, came), (target, goes) in moves:
        keep_ref, got_ref = ins[2 * source], ins[2 * source + 1]
        send_ref, left_ref = outs[2 * target], outs[2 * target + 1]
        count = keep_ref.shape[0]
        mine = (replica_ref[0] // bit) & 1
        at = 0
        for base in range(0, count, 2 * stride):
            for offset in range(stride):
                give = base + offset + stride * (1 - mine)
                hold = base + offset + stride * mine
                send_ref[at, :, goes] = (
                    keep_ref[give, :, came] + got_ref[give, :, came].astype(F32)
                ).astype(BF16)
                left_ref[at, :, goes] = keep_ref[hold, :, came] + got_ref[hold, :, came].astype(F32)
                at += 1


def last_kernel(keep_ref, got_ref, taps_ref, came_ref, point_ref, out_ref):
    point_ref[...] = keep_ref[0] + got_ref[0].astype(F32)
    out_ref[...] = taps_ref[...] + came_ref[...]


def backward_kernel(
    slot_grads_ref, weight_ref, kernel_ref, scaled_ref, inverse_ref, *refs, sizes, side
):
    _, _, sections, capacity = sizes
    slots = sections * capacity
    back_refs, refs = refs[: sections - 1], refs[sections - 1 :]
    grad_in_ref, mixed_ref, work_ref = refs
    work_ref[...] = lax.dot_general(
        slot_grads_ref[...], weight_ref[...], (((1,), (1,)), ((), ())), preferred_element_type=F32
    )
    block = side * slots
    for row in range(side):
        rows = pl.ds(row * block, block)
        scaled = scaled_ref[rows, :]
        logistic = jax.nn.sigmoid(scaled)
        grad_scaled = work_ref[rows, :] * logistic * (1.0 + scaled * (1.0 - logistic))
        mean = jnp.mean(grad_scaled * scaled, axis=-1, keepdims=True)
        mixed_ref[rows, :] = inverse_ref[rows, :1] * (grad_scaled - scaled * mean)

    def emit(rows, lanes, value):
        work_ref[rows, lanes] = value

    correlate(mixed_ref, kernel_ref, side, slots, -1, emit)
    grad_in_ref[...] = (slot_grads_ref[...].astype(F32) + work_ref[...]).astype(BF16)
    return_slots(grad_in_ref[...], back_refs, sizes)


def taps_kernel(at_ref, mixed_ref, source_ref, out_ref, *, side, slots):
    kind = lax.rem(at_ref[0], 3)
    channels = mixed_ref.shape[-1]

    def chunk(at, carry):
        lanes = pl.ds(pl.multiple_of(at * LANES, LANES), LANES)

        def cells(ref, row):
            return [ref[pl.ds((row * side + col) * slots, slots), lanes] for col in range(side)]

        sums = [None] * 25
        for row in range(side):
            grads = cells(mixed_ref, row)
            for row_shift in range(-2, 3):
                if not 0 <= row + row_shift < side:
                    continue
                source = cells(source_ref, row + row_shift)
                for col_shift in range(-2, 3):
                    tap = (row_shift + 2) * 5 + col_shift + 2
                    for col in range(side):
                        if not 0 <= col + col_shift < side:
                            continue
                        term = grads[col] * source[col + col_shift]
                        sums[tap] = term if sums[tap] is None else sums[tap] + term
        for tap in range(25):
            out_ref[tap, :, lanes] = (
                jnp.sum(sums[tap], axis=0, keepdims=True) * tap_keep(kind, tap)
            )
        return carry

    lax.fori_loop(0, channels // LANES, chunk, 0)


def call(kernel, outs, in_specs, scratch=(), megabytes=20):
    return pl.pallas_call(
        kernel,
        out_shape=outs,
        in_specs=in_specs,
        out_specs=jax.tree.map(lambda _: VMEM, outs),
        scratch_shapes=list(scratch),
        compiler_params=pltpu.CompilerParams(vmem_limit_bytes=megabytes * 1024 * 1024),
    )


def window(feature_maps, path_lists, point_weight, depth_kernel, cotangent):
    sections = lax.axis_size("segment")
    ways = lax.axis_size("rep")
    at = lax.axis_index("segment").astype(jnp.int32).reshape(1)
    replica = lax.axis_index("rep").astype(jnp.int32).reshape(1)
    samples, side, _, channels = feature_maps.shape
    places = side * side
    capacity = max(max(2, samples // 4), (samples + sections - 1) // sections)
    slots = sections * capacity
    sizes = (places, samples, sections, capacity)
    path = path_lists[0, :, 0]
    weight = point_weight[0, 0]
    kernel = depth_kernel[0, 0].reshape(25, 1, channels)
    others = range(1, sections)

    def rows_of(maps):
        return jnp.transpose(maps, (1, 2, 0, 3)).reshape(places * samples, channels)

    def maps_of(rows):
        return jnp.transpose(rows.reshape(side, side, samples, channels), (2, 0, 1, 3))

    def shape(*dims, dtype=F32):
        return jax.ShapeDtypeStruct(dims, dtype)

    packed = shape(places * capacity, channels, dtype=BF16)

    def pack(rows, megabytes):
        return call(
            functools.partial(pack_kernel, sizes=sizes),
            [packed for _ in others],
            [SMEM, SMEM, VMEM],
            megabytes=megabytes,
        )(path, at, rows)

    def swap(pieces, direction):
        return [
            lax.ppermute(
                piece,
                "segment",
                [(i, (i + direction * shift) % sections) for i in range(sections)],
            )
            for shift, piece in zip(others, pieces)
        ]

    def unpack(slot_rows, pieces):
        return call(
            functools.partial(unpack_kernel, sizes=sizes),
            shape(places * samples, channels, dtype=BF16),
            [SMEM, SMEM, VMEM] + [VMEM for _ in others],
        )(path, at, slot_rows, *pieces)

    def trade(value, bit):
        return lax.ppermute(value, "rep", [(i, i ^ bit) for i in range(ways)])

    maps, grads = rows_of(feature_maps), rows_of(cotangent)
    got_maps = swap(pack(maps, 56), 1)
    got_grads = swap(pack(grads, 20), 1)

    slot_shape = shape(places * slots, channels)
    slot_half = shape(places * slots, channels, dtype=BF16)
    tap_shape = shape(25, 1, channels)
    own_maps, own_grads, kernel = call(
        functools.partial(prepare_kernel, sizes=sizes),
        [slot_half, slot_half, tap_shape],
        [SMEM, SMEM, VMEM, VMEM, VMEM],
    )(path, at, maps, grads, kernel)
    results = call(
        functools.partial(forward_kernel, sizes=sizes, side=side),
        [packed for _ in others]
        + [slot_half, slot_half, slot_shape, shape(places * slots, LANES), slot_shape],
        [VMEM, VMEM, VMEM] + [VMEM for _ in others],
    )(own_maps, weight, kernel, *got_maps)
    back = results[: sections - 1]
    slot_final, active, scaled, inverse, source = results[sections - 1 :]
    got_final = swap(back, -1)

    block = channels // ways
    slot_grads, send, keep = call(
        functools.partial(point_kernel, sizes=sizes, ways=ways),
        [
            slot_half,
            shape(ways // 2, block, channels, dtype=BF16),
            shape(ways // 2, block, channels),
        ],
        [SMEM, VMEM, VMEM] + [VMEM for _ in others],
        [pltpu.VMEM((ways, block, channels), F32)],
    )(replica, own_grads, active, *got_grads)

    got = trade(send, 1)

    results = call(
        functools.partial(backward_kernel, sizes=sizes, side=side),
        [packed for _ in others] + [slot_half, slot_shape],
        [VMEM, VMEM, VMEM, VMEM, VMEM],
        [pltpu.VMEM((places * slots, channels), F32)],
    )(slot_grads, weight, kernel, scaled, inverse)
    back = results[: sections - 1]
    slot_in, mixed = results[sections - 1 :]
    got_in = swap(back, -1)

    taps = call(
        functools.partial(taps_kernel, side=side, slots=slots), tap_shape, [SMEM, VMEM, VMEM]
    )(at, mixed, source)

    bits = [1 << i for i in range(1, ways.bit_length() - 1)]
    orders = [list(bits), list(bits)]
    if len(bits) > 2:
        orders[1][0], orders[1][1] = bits[1], bits[0]
    half = channels // 2
    halves = [slice(0, half), slice(half, channels)]
    held = [keep, got]
    for step in range(len(bits)):
        first, final = step == 0, step == len(bits) - 1
        count = (ways // 4) >> step
        moves = []
        for part in range(2):
            bit = orders[part][step]
            done = orders[part][:step]
            stride = 1 << sum(1 for other in bits if other < bit and other not in done)
            moves.append(
                (
                    (stride, bit),
                    (0, halves[part]) if first else (part, slice(0, half)),
                    (0, halves[part]) if final else (part, slice(0, half)),
                )
            )
        width, targets = (channels, 1) if final else (half, 2)
        outs = [shape(count, block, width, dtype=BF16), shape(count, block, width)] * targets
        results = call(
            functools.partial(fold_kernel, moves=moves, arriving=len(held)),
            outs,
            [SMEM] + [VMEM] * len(held),
        )(replica, *held)
        held = []
        for part in range(targets):
            held += [results[2 * part + 1], trade(results[2 * part], orders[part][step])]
    tap_bits = [1] + bits[::-1]
    for step, bit in enumerate(tap_bits):
        came = trade(taps, bit)
        if step < len(bits):
            taps = taps + came
    point_grad, taps = call(
        last_kernel, [shape(block, channels), tap_shape], [VMEM] * 4
    )(*held, taps, came)

    final_maps = maps_of(unpack(slot_final, got_final))
    input_grad = maps_of(unpack(slot_in, got_in))
    return (
        final_maps,
        input_grad,
        point_grad.reshape(1, 1, block, channels),
        taps.reshape(1, 1, 25, channels),
    )


def solution(mesh):
    placed = (
        P(("segment", "rep"), None, None, None),
        P(None, ("segment", "rep"), None),
        P(None, "segment", None, None),
        P(None, "segment", None, None),
        P(("segment", "rep"), None, None, None),
    )
    return jax.shard_map(
        window,
        mesh=mesh,
        in_specs=placed,
        out_specs=(
            P(("segment", "rep"), None, None, None),
            P(("segment", "rep"), None, None, None),
            P(None, "segment", "rep", None),
            P(None, "segment", None, None),
        ),
        check_vma=False,
    )
```

```python
import functools

import jax
import jax.numpy as jnp
from jax import lax
from jax.experimental import pallas as pl
from jax.experimental.pallas import tpu as pltpu
from jax.sharding import PartitionSpec as P


EPS = 1e-05
LANES = 128
F32 = jnp.float32
BF16 = jnp.bfloat16

VMEM = pl.BlockSpec(memory_space=pltpu.VMEM)
SMEM = pl.BlockSpec(memory_space=pltpu.SMEM)


def iota2(shape, axis):
    return lax.broadcasted_iota(jnp.int32, shape, axis)


def split(value, size):
    if size & (size - 1) == 0:
        return value >> (size.bit_length() - 1), value & (size - 1)
    quotient = lax.div(value, jnp.int32(size))
    return quotient, value - quotient * size


def slot_codes(path_ref, samples, capacity):
    names = [path_ref[i] for i in range(samples)]
    codes = []
    for i in range(samples):
        rank = jnp.int32(0)
        for j in range(i):
            rank = rank + jnp.where(names[j] == names[i], 1, 0)
        codes.append(names[i] * capacity + rank)
    return codes


def spread_codes(codes, which):
    out = jnp.zeros(which.shape, jnp.int32)
    for i, code in enumerate(codes):
        out = jnp.where(which == i, code, out)
    return out


def one_hot(mask):
    return jnp.where(mask, 1.0, 0.0).astype(BF16)


def pick(matrix, rows):
    return lax.dot_general(matrix, rows, (((1,), (0,)), ((), ())), preferred_element_type=F32)


def pack_matrix(code_row, at, shift, sizes):
    places, samples, sections, capacity = sizes
    row_place, row_slot = split(iota2((places * capacity, places * samples), 0), capacity)
    col_place, _ = split(iota2((1, places * samples), 1), samples)
    target = lax.rem(at + shift, sections)
    return one_hot((row_place == col_place) & (code_row == target * capacity + row_slot))


def first_pack_kernel(path_ref, at_ref, maps_ref, *refs, sizes):
    places, samples, sections, capacity = sizes
    out_refs, code_ref = refs[:-1], refs[-1]
    codes = slot_codes(path_ref, samples, capacity)
    _, col_sample = split(iota2((1, places * samples), 1), samples)
    code_row = spread_codes(codes, col_sample)
    for shift in range(1, sections):
        matrix = pack_matrix(code_row, at_ref[0], shift, sizes)
        out_refs[shift - 1][...] = pick(matrix, maps_ref[...]).astype(BF16)
    code_ref[...] = jnp.broadcast_to(code_row, code_ref.shape)


def second_pack_kernel(code_ref, at_ref, maps_ref, *out_refs, sizes):
    _, _, sections, _ = sizes
    for shift in range(1, sections):
        matrix = pack_matrix(code_ref[:1, :], at_ref[0], shift, sizes)
        out_refs[shift - 1][...] = pick(matrix, maps_ref[...]).astype(BF16)


def prepare_kernel(path_ref, at_ref, code_ref, maps_ref, grads_ref, kernel_ref, *refs, sizes):
    places, samples, sections, capacity = sizes
    slots = sections * capacity
    own_maps_ref, own_grads_ref, taps_ref, place_ref, fetch_ref, home_ref, merge_ref = refs
    row_place, row_slot = split(iota2((places * slots, places * samples), 0), slots)
    col_place, _ = split(iota2((1, places * samples), 1), samples)
    mask = (
        (row_place == col_place)
        & (row_slot < capacity)
        & (code_ref[:1, :] == at_ref[0] * capacity + row_slot)
    )
    matrix = one_hot(mask)
    own_maps_ref[...] = pick(matrix, maps_ref[...]).astype(BF16)
    own_grads_ref[...] = pick(matrix, grads_ref[...]).astype(BF16)
    kind = lax.rem(at_ref[0], 3)
    for tap in range(25):
        taps_ref[tap] = kernel_ref[tap] * tap_keep(kind, tap)

    row_place, row_slot = split(iota2((places * slots, places * capacity), 0), slots)
    col_place, col_slot = split(iota2((1, places * capacity), 1), capacity)
    for shift in range(1, sections):
        mask = (row_place == col_place) & (row_slot == shift * capacity + col_slot)
        place_ref[shift - 1] = one_hot(mask)
    row_place, row_slot = split(iota2((places * capacity, places * slots), 0), capacity)
    col_place, col_slot = split(iota2((1, places * slots), 1), slots)
    for shift in range(1, sections):
        mask = (row_place == col_place) & (col_slot == shift * capacity + row_slot)
        fetch_ref[shift - 1] = one_hot(mask)

    codes = slot_codes(path_ref, samples, capacity)
    row_place, row_sample = split(iota2((places * samples, 1), 0), samples)
    row_code = spread_codes(codes, row_sample)
    col_place, col_slot = split(iota2((1, places * slots), 1), slots)
    mask = (
        (row_place == col_place)
        & (col_slot < capacity)
        & (row_code == at_ref[0] * capacity + col_slot)
    )
    home_ref[...] = one_hot(mask)
    col_place, col_slot = split(iota2((1, places * capacity), 1), capacity)
    for shift in range(1, sections):
        target = lax.rem(at_ref[0] + shift, sections)
        mask = (row_place == col_place) & (row_code == target * capacity + col_slot)
        merge_ref[shift - 1] = one_hot(mask)


def gather_slots(own_ref, place_ref, got_refs):
    total = own_ref[...].astype(F32)
    for at, got_ref in enumerate(got_refs):
        total = total + pick(place_ref[at], got_ref[...])
    return total


def return_slots(slot_rows, fetch_ref, out_refs):
    for at, out_ref in enumerate(out_refs):
        out_ref[...] = pick(fetch_ref[at], slot_rows).astype(BF16)


def unpack_kernel(home_ref, merge_ref, slots_ref, *refs):
    got_refs, out_ref = refs[:-1], refs[-1]
    total = pick(home_ref[...], slots_ref[...])
    for at, got_ref in enumerate(got_refs):
        total = total + pick(merge_ref[at], got_ref[...])
    out_ref[...] = total.astype(BF16)


def tap_keep(kind, tap):
    row_shift, col_shift = tap // 5 - 2, tap % 5 - 2
    narrow = abs(row_shift) <= 1 and abs(col_shift) <= 1
    spaced = row_shift % 2 == 0 and col_shift % 2 == 0
    keep = kind == 1
    if narrow:
        keep = keep | (kind == 0)
    if spaced:
        keep = keep | (kind == 2)
    return jnp.where(keep, 1.0, 0.0).astype(F32)


def correlate(source_ref, kernel_ref, side, slots, sign, emit):
    channels = source_ref.shape[-1]

    def chunk(at, carry):
        lanes = pl.ds(pl.multiple_of(at * LANES, LANES), LANES)
        taps = [
            jnp.broadcast_to(kernel_ref[tap, :, lanes], (slots, LANES)) for tap in range(25)
        ]
        for row in range(side):
            sums = [None] * side
            for row_shift in range(-2, 3):
                source_row = row + sign * row_shift
                if not 0 <= source_row < side:
                    continue
                cells = [
                    source_ref[pl.ds((source_row * side + col) * slots, slots), lanes]
                    for col in range(side)
                ]
                for col_shift in range(-2, 3):
                    tap = taps[(row_shift + 2) * 5 + col_shift + 2]
                    for col in range(side):
                        source_col = col + sign * col_shift
                        if not 0 <= source_col < side:
                            continue
                        term = tap * cells[source_col]
                        sums[col] = term if sums[col] is None else sums[col] + term
            for col in range(side):
                emit(pl.ds((row * side + col) * slots, slots), lanes, sums[col])
        return carry

    lax.fori_loop(0, channels // LANES, chunk, 0)


def deal(replica_ref, rows_ref, give_ref, hold_ref):
    low = replica_ref[0] & 1
    count, block = give_ref.shape[0], give_ref.shape[1]
    for at in range(count):
        give_ref[at] = rows_ref[pl.ds(pl.multiple_of((2 * at + 1 - low) * block, block), block), :]
        hold_ref[at] = rows_ref[pl.ds(pl.multiple_of((2 * at + low) * block, block), block), :]


def forward_kernel(replica_ref, own_ref, place_ref, fetch_ref, weight_ref, kernel_ref, *refs, sizes, side):
    _, _, sections, capacity = sizes
    slots = sections * capacity
    got_refs, refs = refs[: sections - 1], refs[sections - 1 :]
    back_refs, refs = refs[: sections - 1], refs[sections - 1 :]
    give_refs, refs = refs[: sections - 1], refs[sections - 1 :]
    hold_refs, refs = refs[: sections - 1], refs[sections - 1 :]
    final_ref, active_ref, scaled_ref, inverse_ref, source_ref, turned_ref = refs
    source_ref[...] = gather_slots(own_ref, place_ref, got_refs)

    def emit(rows, lanes, value):
        scaled_ref[rows, lanes] = value

    correlate(source_ref, kernel_ref, side, slots, 1, emit)
    block = side * slots
    for row in range(side):
        rows = pl.ds(row * block, block)
        mixed = scaled_ref[rows, :]
        inverse = lax.rsqrt(jnp.mean(mixed * mixed, axis=-1, keepdims=True) + EPS)
        scaled = mixed * inverse
        scaled_ref[rows, :] = scaled
        inverse_ref[rows, :] = jnp.broadcast_to(inverse, (block, LANES))
        active_ref[rows, :] = (scaled * jax.nn.sigmoid(scaled)).astype(BF16)
    branch = pick(active_ref[...], weight_ref[...])
    final_ref[...] = (source_ref[...] + branch).astype(BF16)
    return_slots(final_ref[...], fetch_ref, back_refs)
    for at in range(sections - 1):
        turned = lax.dot_general(
            active_ref[...], fetch_ref[at], (((0,), (1,)), ((), ())), preferred_element_type=F32
        )
        turned_ref[...] = turned.astype(BF16)
        deal(replica_ref, turned_ref, give_refs[at], hold_refs[at])


def own_point_kernel(replica_ref, active_ref, own_ref, give_ref, hold_ref, total_ref):
    total_ref[...] = lax.dot_general(
        active_ref[...], own_ref[...], (((0,), (0,)), ((), ())), preferred_element_type=F32
    )
    deal(replica_ref, total_ref, give_ref, hold_ref)


def point_kernel(own_ref, *refs):
    out_ref = refs[-1]
    active_refs, got_refs = refs[: len(refs) // 2], refs[len(refs) // 2 : -1]
    shape = own_ref.shape
    total = own_ref[...].reshape(shape[0] * shape[1], shape[2])
    for active_ref, got_ref in zip(active_refs, got_refs):
        active = active_ref[...].reshape(shape[0] * shape[1], active_ref.shape[2])
        total = total + pick(active, got_ref[...])
    out_ref[...] = total.reshape(shape).astype(out_ref.dtype)


def fold_kernel(replica_ref, keep_ref, got_ref, send_ref, left_ref, *, strides, bits):
    core = replica_ref[0] & 1
    mine = jnp.where(core == 0, (replica_ref[0] // bits[0]) & 1, (replica_ref[0] // bits[1]) & 1)
    for at in range(send_ref.shape[0]):
        low, high = [(at // stride) * 2 * stride + at % stride for stride in strides]
        base = jnp.where(core == 0, low, high)
        step = jnp.where(core == 0, strides[0], strides[1])
        give = base + step * (1 - mine)
        hold = base + step * mine
        send_ref[at] = (keep_ref[give] + got_ref[give].astype(F32)).astype(BF16)
        left_ref[at] = keep_ref[hold] + got_ref[hold].astype(F32)


def last_kernel(replica_ref, keep_ref, got_ref, taps_ref, came_ref, point_ref, out_ref):
    point_ref[...] = keep_ref[0] + got_ref[0].astype(F32)
    core = replica_ref[0] & 1
    half = taps_ref.shape[-1]
    out_ref[:, :, pl.ds(pl.multiple_of(core * half, LANES), half)] = taps_ref[...]
    out_ref[:, :, pl.ds(pl.multiple_of((1 - core) * half, LANES), half)] = came_ref[...]


def mixed_kernel(own_ref, place_ref, weight_ref, scaled_ref, inverse_ref, *refs, block):
    got_refs, (slot_grads_ref, mixed_ref, work_ref) = refs[:-3], refs[-3:]
    slot_grads_ref[...] = gather_slots(own_ref, place_ref, got_refs).astype(BF16)
    work_ref[...] = lax.dot_general(
        slot_grads_ref[...], weight_ref[...], (((1,), (1,)), ((), ())), preferred_element_type=F32
    )
    for at in range(0, work_ref.shape[0], block):
        rows = pl.ds(at, block)
        scaled = scaled_ref[rows, :]
        logistic = jax.nn.sigmoid(scaled)
        grad_scaled = work_ref[rows, :] * logistic * (1.0 + scaled * (1.0 - logistic))
        mean = jnp.mean(grad_scaled * scaled, axis=-1, keepdims=True)
        mixed_ref[rows, :] = inverse_ref[rows, :1] * (grad_scaled - scaled * mean)


def backward_kernel(slot_grads_ref, fetch_ref, kernel_ref, mixed_ref, *refs, side, slots):
    back_refs, grad_in_ref, work_ref = refs[:-2], refs[-2], refs[-1]

    def emit(rows, lanes, value):
        work_ref[rows, lanes] = value

    correlate(mixed_ref, kernel_ref, side, slots, -1, emit)
    grad_in_ref[...] = (slot_grads_ref[...].astype(F32) + work_ref[...]).astype(BF16)
    return_slots(grad_in_ref[...], fetch_ref, back_refs)


def taps_kernel(at_ref, replica_ref, mixed_ref, source_ref, out_ref, *, side, slots, flip):
    kind = lax.rem(at_ref[0], 3)
    half = out_ref.shape[-1]
    which = (replica_ref[0] & 1) ^ flip

    def chunk(at, carry):
        lanes = pl.ds(pl.multiple_of(which * half + at * LANES, LANES), LANES)
        target = pl.ds(pl.multiple_of(at * LANES, LANES), LANES)

        def cells(ref, row):
            return [ref[pl.ds((row * side + col) * slots, slots), lanes] for col in range(side)]

        sums = [None] * 25
        for row in range(side):
            grads = cells(mixed_ref, row)
            for row_shift in range(-2, 3):
                if not 0 <= row + row_shift < side:
                    continue
                source = cells(source_ref, row + row_shift)
                for col_shift in range(-2, 3):
                    tap = (row_shift + 2) * 5 + col_shift + 2
                    for col in range(side):
                        if not 0 <= col + col_shift < side:
                            continue
                        term = grads[col] * source[col + col_shift]
                        sums[tap] = term if sums[tap] is None else sums[tap] + term
        for tap in range(25):
            out_ref[tap, :, target] = (
                jnp.sum(sums[tap], axis=0, keepdims=True) * tap_keep(kind, tap)
            )
        return carry

    lax.fori_loop(0, half // LANES, chunk, 0)


def call(kernel, outs, in_specs, scratch=(), megabytes=20):
    return pl.pallas_call(
        kernel,
        out_shape=outs,
        in_specs=in_specs,
        out_specs=jax.tree.map(lambda _: VMEM, outs),
        scratch_shapes=list(scratch),
        compiler_params=pltpu.CompilerParams(vmem_limit_bytes=megabytes * 1024 * 1024),
    )


def window(feature_maps, path_lists, point_weight, depth_kernel, cotangent):
    sections = lax.axis_size("segment")
    ways = lax.axis_size("rep")
    at = lax.axis_index("segment").astype(jnp.int32).reshape(1)
    replica = lax.axis_index("rep").astype(jnp.int32).reshape(1)
    samples, side, _, channels = feature_maps.shape
    places = side * side
    capacity = max(max(2, samples // 4), (samples + sections - 1) // sections)
    slots = sections * capacity
    sizes = (places, samples, sections, capacity)
    path = path_lists[0, :, 0]
    weight = point_weight[0, 0]
    kernel = depth_kernel[0, 0].reshape(25, 1, channels)
    others = range(1, sections)

    def rows_of(maps):
        return jnp.transpose(maps, (1, 2, 0, 3)).reshape(places * samples, channels)

    def maps_of(rows):
        return jnp.transpose(rows.reshape(side, side, samples, channels), (2, 0, 1, 3))

    def shape(*dims, dtype=F32):
        return jax.ShapeDtypeStruct(dims, dtype)

    packed = shape(places * capacity, channels, dtype=BF16)

    def swap(pieces, direction):
        return [
            lax.ppermute(
                piece,
                "segment",
                [(i, (i + direction * shift) % sections) for i in range(sections)],
            )
            for shift, piece in zip(others, pieces)
        ]

    def unpack(slot_rows, pieces):
        return call(
            unpack_kernel, shape(places * samples, channels, dtype=BF16), [VMEM] * (3 + len(pieces))
        )(home, merge, slot_rows, *pieces)

    def trade(value, pair):
        return lax.ppermute(value, "rep", [(i, i ^ pair[i & 1]) for i in range(ways)])

    maps, grads = rows_of(feature_maps), rows_of(cotangent)
    code_shape = jax.ShapeDtypeStruct((8, places * samples), jnp.int32)
    *packs, code_row = call(
        functools.partial(first_pack_kernel, sizes=sizes),
        [packed for _ in others] + [code_shape],
        [SMEM, SMEM, VMEM],
        megabytes=56,
    )(path, at, maps)
    got_maps = swap(packs, 1)
    packs = call(
        functools.partial(second_pack_kernel, sizes=sizes),
        [packed for _ in others],
        [VMEM, SMEM, VMEM],
    )(code_row, at, grads)
    got_grads = swap(packs, 1)

    slot_shape = shape(places * slots, channels)
    slot_half = shape(places * slots, channels, dtype=BF16)
    tap_shape = shape(25, 1, channels)
    own_maps, own_grads, kernel, place, fetch, home, merge = call(
        functools.partial(prepare_kernel, sizes=sizes),
        [
            slot_half,
            slot_half,
            tap_shape,
            shape(sections - 1, places * slots, places * capacity, dtype=BF16),
            shape(sections - 1, places * capacity, places * slots, dtype=BF16),
            shape(places * samples, places * slots, dtype=BF16),
            shape(sections - 1, places * samples, places * capacity, dtype=BF16),
        ],
        [SMEM, SMEM, VMEM, VMEM, VMEM, VMEM],
    )(path, at, code_row, maps, grads, kernel)
    block = channels // ways
    turned = shape(ways // 2, block, places * capacity, dtype=BF16)
    results = call(
        functools.partial(forward_kernel, sizes=sizes, side=side),
        [packed for _ in others]
        + [turned for _ in others] * 2
        + [slot_half, slot_half, slot_shape, shape(places * slots, LANES), slot_shape],
        [SMEM] + [VMEM] * (5 + len(got_maps)),
        [pltpu.VMEM((channels, places * capacity), BF16)],
    )(replica, own_maps, place, fetch, weight, kernel, *got_maps)
    count = sections - 1
    back, active_give, active_hold = [results[i * count : (i + 1) * count] for i in range(3)]
    slot_final, active, scaled, inverse, source = results[3 * count :]

    part = shape(ways // 2, block, channels)
    own_give, own_hold = call(
        own_point_kernel, [part, part], [SMEM, VMEM, VMEM], [pltpu.VMEM((channels, channels), F32)]
    )(replica, active, own_grads)
    got_final = swap(back, -1)

    send = call(
        point_kernel, shape(ways // 2, block, channels, dtype=BF16), [VMEM] * (1 + 2 * count)
    )(own_give, *active_give, *got_grads)
    got = trade(send, (1, 1))
    keep = call(point_kernel, part, [VMEM] * (1 + 2 * count))(own_hold, *active_hold, *got_grads)

    slot_grads, mixed = call(
        functools.partial(mixed_kernel, block=side * slots),
        [slot_half, slot_shape],
        [VMEM] * (5 + len(got_grads)),
        [pltpu.VMEM((places * slots, channels), F32)],
    )(own_grads, place, weight, scaled, inverse, *got_grads)
    *back, slot_in = call(
        functools.partial(backward_kernel, side=side, slots=slots),
        [packed for _ in others] + [slot_half],
        [VMEM] * 4,
        [pltpu.VMEM((places * slots, channels), F32)],
    )(slot_grads, fetch, kernel, mixed)
    got_in = swap(back, -1)

    half_shape = shape(25, 1, channels // 2)

    def tap_sums(flip):
        return call(
            functools.partial(taps_kernel, side=side, slots=slots, flip=flip),
            half_shape,
            [SMEM, SMEM, VMEM, VMEM],
        )(at, replica, mixed, source)

    give, taps = tap_sums(1), tap_sums(0)

    bits = [1 << i for i in range(1, ways.bit_length() - 1)]
    swapped = bits[1::-1] + bits[2:] if len(bits) > 2 else bits
    for step, pair in enumerate(zip(bits, swapped)):
        count = (ways // 4) >> step
        strides = []
        for order in (bits, swapped):
            done = order[:step]
            strides.append(1 << sum(1 for other in bits if other < order[step] and other not in done))
        send, keep = call(
            functools.partial(fold_kernel, strides=strides, bits=pair),
            [shape(count, block, channels, dtype=BF16), shape(count, block, channels)],
            [SMEM, VMEM, VMEM],
        )(replica, keep, got)
        got = trade(send, pair)

    later = bits[:-1]
    pairs = [(1, 1), (bits[-1], bits[-1])] + list(zip(later, later[1:] + later[:1]))
    for step, pair in enumerate(pairs):
        came = trade(give if step == 0 else taps, pair)
        taps = taps + came
    came = trade(taps, (1, 1))
    point_grad, taps = call(
        last_kernel, [shape(block, channels), tap_shape], [SMEM] + [VMEM] * 4
    )(replica, keep, got, taps, came)

    final_maps = maps_of(unpack(slot_final, got_final))
    input_grad = maps_of(unpack(slot_in, got_in))
    return (
        final_maps,
        input_grad,
        point_grad.reshape(1, 1, block, channels),
        taps.reshape(1, 1, 25, channels),
    )


def solution(mesh):
    placed = (
        P(("segment", "rep"), None, None, None),
        P(None, ("segment", "rep"), None),
        P(None, "segment", None, None),
        P(None, "segment", None, None),
        P(("segment", "rep"), None, None, None),
    )
    return jax.shard_map(
        window,
        mesh=mesh,
        in_specs=placed,
        out_specs=(
            P(("segment", "rep"), None, None, None),
            P(("segment", "rep"), None, None, None),
            P(None, "segment", "rep", None),
            P(None, "segment", None, None),
        ),
        check_vma=False,
    )
```

```python
import functools

import jax
import jax.numpy as jnp
from jax import lax
from jax.experimental import pallas as pl
from jax.experimental.pallas import tpu as pltpu
from jax.sharding import PartitionSpec as P


EPS = 1e-05
LANES = 128
F32 = jnp.float32
BF16 = jnp.bfloat16

VMEM = pl.BlockSpec(memory_space=pltpu.VMEM)
SMEM = pl.BlockSpec(memory_space=pltpu.SMEM)


def iota2(shape, axis):
    return lax.broadcasted_iota(jnp.int32, shape, axis)


def split(value, size):
    if size & (size - 1) == 0:
        return value >> (size.bit_length() - 1), value & (size - 1)
    quotient = lax.div(value, jnp.int32(size))
    return quotient, value - quotient * size


def slot_codes(path_ref, samples, capacity):
    names = [path_ref[i] for i in range(samples)]
    codes = []
    for i in range(samples):
        rank = jnp.int32(0)
        for j in range(i):
            rank = rank + jnp.where(names[j] == names[i], 1, 0)
        codes.append(names[i] * capacity + rank)
    return codes


def spread_codes(codes, which):
    out = jnp.zeros(which.shape, jnp.int32)
    for i, code in enumerate(codes):
        out = jnp.where(which == i, code, out)
    return out


def one_hot(mask):
    return jnp.where(mask, 1.0, 0.0).astype(BF16)


def pick(matrix, rows):
    return lax.dot_general(matrix, rows, (((1,), (0,)), ((), ())), preferred_element_type=F32)


def pack_matrix(code_row, at, shift, sizes):
    places, samples, sections, capacity = sizes
    row_place, row_slot = split(iota2((places * capacity, places * samples), 0), capacity)
    col_place, _ = split(iota2((1, places * samples), 1), samples)
    target = lax.rem(at + shift, sections)
    return one_hot((row_place == col_place) & (code_row == target * capacity + row_slot))


def first_pack_kernel(path_ref, at_ref, maps_ref, *refs, sizes):
    places, samples, sections, capacity = sizes
    out_refs, code_ref = refs[:-1], refs[-1]
    codes = slot_codes(path_ref, samples, capacity)
    _, col_sample = split(iota2((1, places * samples), 1), samples)
    code_row = spread_codes(codes, col_sample)
    for shift in range(1, sections):
        matrix = pack_matrix(code_row, at_ref[0], shift, sizes)
        out_refs[shift - 1][...] = pick(matrix, maps_ref[...]).astype(BF16)
    code_ref[...] = jnp.broadcast_to(code_row, code_ref.shape)


def second_pack_kernel(code_ref, at_ref, maps_ref, *out_refs, sizes):
    _, _, sections, _ = sizes
    for shift in range(1, sections):
        matrix = pack_matrix(code_ref[:1, :], at_ref[0], shift, sizes)
        out_refs[shift - 1][...] = pick(matrix, maps_ref[...]).astype(BF16)


def prepare_kernel(path_ref, at_ref, code_ref, maps_ref, grads_ref, kernel_ref, *refs, sizes):
    places, samples, sections, capacity = sizes
    slots = sections * capacity
    own_maps_ref, own_grads_ref, taps_ref, place_ref, fetch_ref, home_ref, merge_ref = refs
    row_place, row_slot = split(iota2((places * slots, places * samples), 0), slots)
    col_place, _ = split(iota2((1, places * samples), 1), samples)
    mask = (
        (row_place == col_place)
        & (row_slot < capacity)
        & (code_ref[:1, :] == at_ref[0] * capacity + row_slot)
    )
    matrix = one_hot(mask)
    own_maps_ref[...] = pick(matrix, maps_ref[...]).astype(BF16)
    own_grads_ref[...] = pick(matrix, grads_ref[...]).astype(BF16)
    kind = lax.rem(at_ref[0], 3)
    for tap in range(25):
        taps_ref[tap] = kernel_ref[tap] * tap_keep(kind, tap)

    row_place, row_slot = split(iota2((places * slots, places * capacity), 0), slots)
    col_place, col_slot = split(iota2((1, places * capacity), 1), capacity)
    for shift in range(1, sections):
        mask = (row_place == col_place) & (row_slot == shift * capacity + col_slot)
        place_ref[shift - 1] = one_hot(mask)
    row_place, row_slot = split(iota2((places * capacity, places * slots), 0), capacity)
    col_place, col_slot = split(iota2((1, places * slots), 1), slots)
    for shift in range(1, sections):
        mask = (row_place == col_place) & (col_slot == shift * capacity + row_slot)
        fetch_ref[shift - 1] = one_hot(mask)

    codes = slot_codes(path_ref, samples, capacity)
    row_place, row_sample = split(iota2((places * samples, 1), 0), samples)
    row_code = spread_codes(codes, row_sample)
    col_place, col_slot = split(iota2((1, places * slots), 1), slots)
    mask = (
        (row_place == col_place)
        & (col_slot < capacity)
        & (row_code == at_ref[0] * capacity + col_slot)
    )
    home_ref[...] = one_hot(mask)
    col_place, col_slot = split(iota2((1, places * capacity), 1), capacity)
    for shift in range(1, sections):
        target = lax.rem(at_ref[0] + shift, sections)
        mask = (row_place == col_place) & (row_code == target * capacity + col_slot)
        merge_ref[shift - 1] = one_hot(mask)


def gather_slots(own_ref, place_ref, got_refs):
    total = own_ref[...].astype(F32)
    for at, got_ref in enumerate(got_refs):
        total = total + pick(place_ref[at], got_ref[...])
    return total


def return_slots(slot_rows, fetch_ref, out_refs):
    for at, out_ref in enumerate(out_refs):
        out_ref[...] = pick(fetch_ref[at], slot_rows).astype(BF16)


def unpack_kernel(home_ref, merge_ref, slots_ref, *refs):
    got_refs, out_ref = refs[:-1], refs[-1]
    total = pick(home_ref[...], slots_ref[...])
    for at, got_ref in enumerate(got_refs):
        total = total + pick(merge_ref[at], got_ref[...])
    out_ref[...] = total.astype(BF16)


def tap_keep(kind, tap):
    row_shift, col_shift = tap // 5 - 2, tap % 5 - 2
    narrow = abs(row_shift) <= 1 and abs(col_shift) <= 1
    spaced = row_shift % 2 == 0 and col_shift % 2 == 0
    keep = kind == 1
    if narrow:
        keep = keep | (kind == 0)
    if spaced:
        keep = keep | (kind == 2)
    return jnp.where(keep, 1.0, 0.0).astype(F32)


def correlate(source_ref, kernel_ref, side, slots, sign, emit):
    channels = source_ref.shape[-1]

    def chunk(at, carry):
        lanes = pl.ds(pl.multiple_of(at * LANES, LANES), LANES)
        taps = [
            jnp.broadcast_to(kernel_ref[tap, :, lanes], (slots, LANES)) for tap in range(25)
        ]
        for row in range(side):
            sums = [None] * side
            for row_shift in range(-2, 3):
                source_row = row + sign * row_shift
                if not 0 <= source_row < side:
                    continue
                cells = [
                    source_ref[pl.ds((source_row * side + col) * slots, slots), lanes]
                    for col in range(side)
                ]
                for col_shift in range(-2, 3):
                    tap = taps[(row_shift + 2) * 5 + col_shift + 2]
                    for col in range(side):
                        source_col = col + sign * col_shift
                        if not 0 <= source_col < side:
                            continue
                        term = tap * cells[source_col]
                        sums[col] = term if sums[col] is None else sums[col] + term
            for col in range(side):
                emit(pl.ds((row * side + col) * slots, slots), lanes, sums[col])
        return carry

    lax.fori_loop(0, channels // LANES, chunk, 0)


def deal(replica_ref, rows_ref, give_ref, hold_ref):
    low = replica_ref[0] & 1
    count, block = give_ref.shape[0], give_ref.shape[1]
    for at in range(count):
        give_ref[at] = rows_ref[pl.ds(pl.multiple_of((2 * at + 1 - low) * block, block), block), :]
        hold_ref[at] = rows_ref[pl.ds(pl.multiple_of((2 * at + low) * block, block), block), :]


def forward_kernel(replica_ref, own_ref, place_ref, fetch_ref, weight_ref, kernel_ref, *refs, sizes, side):
    _, _, sections, capacity = sizes
    slots = sections * capacity
    got_refs, refs = refs[: sections - 1], refs[sections - 1 :]
    back_refs, refs = refs[: sections - 1], refs[sections - 1 :]
    give_refs, refs = refs[: sections - 1], refs[sections - 1 :]
    hold_refs, refs = refs[: sections - 1], refs[sections - 1 :]
    final_ref, active_ref, scaled_ref, inverse_ref, source_ref, turned_ref = refs
    source_ref[...] = gather_slots(own_ref, place_ref, got_refs)

    def emit(rows, lanes, value):
        scaled_ref[rows, lanes] = value

    correlate(source_ref, kernel_ref, side, slots, 1, emit)
    block = side * slots
    for row in range(side):
        rows = pl.ds(row * block, block)
        mixed = scaled_ref[rows, :]
        inverse = lax.rsqrt(jnp.mean(mixed * mixed, axis=-1, keepdims=True) + EPS)
        scaled = mixed * inverse
        scaled_ref[rows, :] = scaled
        inverse_ref[rows, :] = jnp.broadcast_to(inverse, (block, LANES))
        active_ref[rows, :] = (scaled * jax.nn.sigmoid(scaled)).astype(BF16)
    branch = pick(active_ref[...], weight_ref[...])
    final_ref[...] = (source_ref[...] + branch).astype(BF16)
    return_slots(final_ref[...], fetch_ref, back_refs)
    for at in range(sections - 1):
        turned = lax.dot_general(
            active_ref[...], fetch_ref[at], (((0,), (1,)), ((), ())), preferred_element_type=F32
        )
        turned_ref[...] = turned.astype(BF16)
        deal(replica_ref, turned_ref, give_refs[at], hold_refs[at])


def own_point_kernel(replica_ref, active_ref, own_ref, give_ref, hold_ref, total_ref):
    total_ref[...] = lax.dot_general(
        active_ref[...], own_ref[...], (((0,), (0,)), ((), ())), preferred_element_type=F32
    )
    deal(replica_ref, total_ref, give_ref, hold_ref)


def point_kernel(own_ref, *refs):
    out_ref = refs[-1]
    active_refs, got_refs = refs[: len(refs) // 2], refs[len(refs) // 2 : -1]
    shape = own_ref.shape
    total = own_ref[...].reshape(shape[0] * shape[1], shape[2])
    for active_ref, got_ref in zip(active_refs, got_refs):
        active = active_ref[...].reshape(shape[0] * shape[1], active_ref.shape[2])
        total = total + pick(active, got_ref[...])
    out_ref[...] = total.reshape(shape).astype(out_ref.dtype)


def fold_kernel(replica_ref, keep_ref, got_ref, send_ref, left_ref, *, strides, bits):
    core = replica_ref[0] & 1
    mine = jnp.where(core == 0, (replica_ref[0] // bits[0]) & 1, (replica_ref[0] // bits[1]) & 1)
    for at in range(send_ref.shape[0]):
        low, high = [(at // stride) * 2 * stride + at % stride for stride in strides]
        base = jnp.where(core == 0, low, high)
        step = jnp.where(core == 0, strides[0], strides[1])
        give = base + step * (1 - mine)
        hold = base + step * mine
        send_ref[at] = (keep_ref[give] + got_ref[give].astype(F32)).astype(BF16)
        left_ref[at] = keep_ref[hold] + got_ref[hold].astype(F32)


def last_kernel(replica_ref, keep_ref, got_ref, taps_ref, came_ref, point_ref, out_ref):
    point_ref[...] = keep_ref[0] + got_ref[0].astype(F32)
    core = replica_ref[0] & 1
    half = taps_ref.shape[-1]
    out_ref[:, :, pl.ds(pl.multiple_of(core * half, LANES), half)] = taps_ref[...]
    out_ref[:, :, pl.ds(pl.multiple_of((1 - core) * half, LANES), half)] = came_ref[...]


def mixed_kernel(own_ref, place_ref, weight_ref, scaled_ref, inverse_ref, *refs, block):
    got_refs, (slot_grads_ref, mixed_ref, work_ref) = refs[:-3], refs[-3:]
    slot_grads_ref[...] = gather_slots(own_ref, place_ref, got_refs).astype(BF16)
    work_ref[...] = lax.dot_general(
        slot_grads_ref[...], weight_ref[...], (((1,), (1,)), ((), ())), preferred_element_type=F32
    )
    for at in range(0, work_ref.shape[0], block):
        rows = pl.ds(at, block)
        scaled = scaled_ref[rows, :]
        logistic = jax.nn.sigmoid(scaled)
        grad_scaled = work_ref[rows, :] * logistic * (1.0 + scaled * (1.0 - logistic))
        mean = jnp.mean(grad_scaled * scaled, axis=-1, keepdims=True)
        mixed_ref[rows, :] = inverse_ref[rows, :1] * (grad_scaled - scaled * mean)


def backward_kernel(slot_grads_ref, fetch_ref, kernel_ref, mixed_ref, *refs, side, slots):
    back_refs, grad_in_ref, work_ref = refs[:-2], refs[-2], refs[-1]

    def emit(rows, lanes, value):
        work_ref[rows, lanes] = value

    correlate(mixed_ref, kernel_ref, side, slots, -1, emit)
    grad_in_ref[...] = (slot_grads_ref[...].astype(F32) + work_ref[...]).astype(BF16)
    return_slots(grad_in_ref[...], fetch_ref, back_refs)


def taps_kernel(at_ref, replica_ref, mixed_ref, source_ref, out_ref, *, side, slots, flip):
    kind = lax.rem(at_ref[0], 3)
    half = out_ref.shape[-1]
    which = (replica_ref[0] & 1) ^ flip

    def chunk(at, carry):
        lanes = pl.ds(pl.multiple_of(which * half + at * LANES, LANES), LANES)
        target = pl.ds(pl.multiple_of(at * LANES, LANES), LANES)

        def cells(ref, row):
            return [ref[pl.ds((row * side + col) * slots, slots), lanes] for col in range(side)]

        sums = [None] * 25
        for row in range(side):
            grads = cells(mixed_ref, row)
            for row_shift in range(-2, 3):
                if not 0 <= row + row_shift < side:
                    continue
                source = cells(source_ref, row + row_shift)
                for col_shift in range(-2, 3):
                    tap = (row_shift + 2) * 5 + col_shift + 2
                    terms = [
                        grads[col] * source[col + col_shift]
                        for col in range(side)
                        if 0 <= col + col_shift < side
                    ]
                    while len(terms) > 1:
                        terms = [sum(terms[i + 1 : i + 2], terms[i]) for i in range(0, len(terms), 2)]
                    sums[tap] = terms[0] if sums[tap] is None else sums[tap] + terms[0]
        for tap in range(25):
            out_ref[tap, :, target] = (
                jnp.sum(sums[tap], axis=0, keepdims=True) * tap_keep(kind, tap)
            )
        return carry

    lax.fori_loop(0, half // LANES, chunk, 0)


def call(kernel, outs, in_specs, scratch=(), megabytes=20):
    return pl.pallas_call(
        kernel,
        out_shape=outs,
        in_specs=in_specs,
        out_specs=jax.tree.map(lambda _: VMEM, outs),
        scratch_shapes=list(scratch),
        compiler_params=pltpu.CompilerParams(vmem_limit_bytes=megabytes * 1024 * 1024),
    )


def window(feature_maps, path_lists, point_weight, depth_kernel, cotangent):
    sections = lax.axis_size("segment")
    ways = lax.axis_size("rep")
    at = lax.axis_index("segment").astype(jnp.int32).reshape(1)
    replica = lax.axis_index("rep").astype(jnp.int32).reshape(1)
    samples, side, _, channels = feature_maps.shape
    places = side * side
    capacity = max(max(2, samples // 4), (samples + sections - 1) // sections)
    slots = sections * capacity
    sizes = (places, samples, sections, capacity)
    path = path_lists[0, :, 0]
    weight = point_weight[0, 0]
    kernel = depth_kernel[0, 0].reshape(25, 1, channels)
    others = range(1, sections)

    def rows_of(maps):
        return jnp.transpose(maps, (1, 2, 0, 3)).reshape(places * samples, channels)

    def maps_of(rows):
        return jnp.transpose(rows.reshape(side, side, samples, channels), (2, 0, 1, 3))

    def shape(*dims, dtype=F32):
        return jax.ShapeDtypeStruct(dims, dtype)

    packed = shape(places * capacity, channels, dtype=BF16)

    def swap(pieces, direction):
        return [
            lax.ppermute(
                piece,
                "segment",
                [(i, (i + direction * shift) % sections) for i in range(sections)],
            )
            for shift, piece in zip(others, pieces)
        ]

    def unpack(slot_rows, pieces):
        return call(
            unpack_kernel, shape(places * samples, channels, dtype=BF16), [VMEM] * (3 + len(pieces))
        )(home, merge, slot_rows, *pieces)

    def trade(value, pair):
        return lax.ppermute(value, "rep", [(i, i ^ pair[i & 1]) for i in range(ways)])

    maps, grads = rows_of(feature_maps), rows_of(cotangent)
    code_shape = jax.ShapeDtypeStruct((8, places * samples), jnp.int32)
    *packs, code_row = call(
        functools.partial(first_pack_kernel, sizes=sizes),
        [packed for _ in others] + [code_shape],
        [SMEM, SMEM, VMEM],
        megabytes=56,
    )(path, at, maps)
    got_maps = swap(packs, 1)
    packs = call(
        functools.partial(second_pack_kernel, sizes=sizes),
        [packed for _ in others],
        [VMEM, SMEM, VMEM],
    )(code_row, at, grads)
    got_grads = swap(packs, 1)

    slot_shape = shape(places * slots, channels)
    slot_half = shape(places * slots, channels, dtype=BF16)
    tap_shape = shape(25, 1, channels)
    own_maps, own_grads, kernel, place, fetch, home, merge = call(
        functools.partial(prepare_kernel, sizes=sizes),
        [
            slot_half,
            slot_half,
            tap_shape,
            shape(sections - 1, places * slots, places * capacity, dtype=BF16),
            shape(sections - 1, places * capacity, places * slots, dtype=BF16),
            shape(places * samples, places * slots, dtype=BF16),
            shape(sections - 1, places * samples, places * capacity, dtype=BF16),
        ],
        [SMEM, SMEM, VMEM, VMEM, VMEM, VMEM],
    )(path, at, code_row, maps, grads, kernel)
    block = channels // ways
    turned = shape(ways // 2, block, places * capacity, dtype=BF16)
    results = call(
        functools.partial(forward_kernel, sizes=sizes, side=side),
        [packed for _ in others]
        + [turned for _ in others] * 2
        + [slot_half, slot_half, slot_shape, shape(places * slots, LANES), slot_shape],
        [SMEM] + [VMEM] * (5 + len(got_maps)),
        [pltpu.VMEM((channels, places * capacity), BF16)],
    )(replica, own_maps, place, fetch, weight, kernel, *got_maps)
    count = sections - 1
    back, active_give, active_hold = [results[i * count : (i + 1) * count] for i in range(3)]
    slot_final, active, scaled, inverse, source = results[3 * count :]

    part = shape(ways // 2, block, channels)
    own_give, own_hold = call(
        own_point_kernel, [part, part], [SMEM, VMEM, VMEM], [pltpu.VMEM((channels, channels), F32)]
    )(replica, active, own_grads)
    got_final = swap(back, -1)

    send = call(
        point_kernel, shape(ways // 2, block, channels, dtype=BF16), [VMEM] * (1 + 2 * count)
    )(own_give, *active_give, *got_grads)
    got = trade(send, (1, 1))
    keep = call(point_kernel, part, [VMEM] * (1 + 2 * count))(own_hold, *active_hold, *got_grads)

    slot_grads, mixed = call(
        functools.partial(mixed_kernel, block=side * slots),
        [slot_half, slot_shape],
        [VMEM] * (5 + len(got_grads)),
        [pltpu.VMEM((places * slots, channels), F32)],
    )(own_grads, place, weight, scaled, inverse, *got_grads)
    *back, slot_in = call(
        functools.partial(backward_kernel, side=side, slots=slots),
        [packed for _ in others] + [slot_half],
        [VMEM] * 4,
        [pltpu.VMEM((places * slots, channels), F32)],
    )(slot_grads, fetch, kernel, mixed)
    got_in = swap(back, -1)

    half_shape = shape(25, 1, channels // 2)

    def tap_sums(flip):
        return call(
            functools.partial(taps_kernel, side=side, slots=slots, flip=flip),
            half_shape,
            [SMEM, SMEM, VMEM, VMEM],
        )(at, replica, mixed, source)

    give, taps = tap_sums(1), tap_sums(0)

    bits = [1 << i for i in range(1, ways.bit_length() - 1)]
    swapped = bits[1::-1] + bits[2:] if len(bits) > 2 else bits
    for step, pair in enumerate(zip(bits, swapped)):
        count = (ways // 4) >> step
        strides = []
        for order in (bits, swapped):
            done = order[:step]
            strides.append(1 << sum(1 for other in bits if other < order[step] and other not in done))
        send, keep = call(
            functools.partial(fold_kernel, strides=strides, bits=pair),
            [shape(count, block, channels, dtype=BF16), shape(count, block, channels)],
            [SMEM, VMEM, VMEM],
        )(replica, keep, got)
        got = trade(send, pair)

    later = bits[:-1]
    pairs = [(1, 1), (bits[-1], bits[-1])] + list(zip(later, later[1:] + later[:1]))
    for step, pair in enumerate(pairs):
        came = trade(give if step == 0 else taps, pair)
        taps = taps + came
    came = trade(taps, (1, 1))
    point_grad, taps = call(
        last_kernel, [shape(block, channels), tap_shape], [SMEM] + [VMEM] * 4
    )(replica, keep, got, taps, came)

    final_maps = maps_of(unpack(slot_final, got_final))
    input_grad = maps_of(unpack(slot_in, got_in))
    return (
        final_maps,
        input_grad,
        point_grad.reshape(1, 1, block, channels),
        taps.reshape(1, 1, 25, channels),
    )


def solution(mesh):
    placed = (
        P(("segment", "rep"), None, None, None),
        P(None, ("segment", "rep"), None),
        P(None, "segment", None, None),
        P(None, "segment", None, None),
        P(("segment", "rep"), None, None, None),
    )
    return jax.shard_map(
        window,
        mesh=mesh,
        in_specs=placed,
        out_specs=(
            P(("segment", "rep"), None, None, None),
            P(("segment", "rep"), None, None, None),
            P(None, "segment", "rep", None),
            P(None, "segment", None, None),
        ),
        check_vma=False,
    )
```

```python
import functools

import jax
import jax.numpy as jnp
from jax import lax
from jax.experimental import pallas as pl
from jax.experimental.pallas import tpu as pltpu
from jax.sharding import PartitionSpec as P


EPS = 1e-05
LANES = 128
F32 = jnp.float32
BF16 = jnp.bfloat16

VMEM = pl.BlockSpec(memory_space=pltpu.VMEM)
SMEM = pl.BlockSpec(memory_space=pltpu.SMEM)


def iota2(shape, axis):
    return lax.broadcasted_iota(jnp.int32, shape, axis)


def split(value, size):
    if size & (size - 1) == 0:
        return value >> (size.bit_length() - 1), value & (size - 1)
    quotient = lax.div(value, jnp.int32(size))
    return quotient, value - quotient * size


def slot_codes(path_ref, samples, capacity):
    names = [path_ref[i] for i in range(samples)]
    codes = []
    for i in range(samples):
        rank = jnp.int32(0)
        for j in range(i):
            rank = rank + jnp.where(names[j] == names[i], 1, 0)
        codes.append(names[i] * capacity + rank)
    return codes


def spread_codes(codes, which):
    out = jnp.zeros(which.shape, jnp.int32)
    for i, code in enumerate(codes):
        out = jnp.where(which == i, code, out)
    return out


def one_hot(mask):
    return jnp.where(mask, 1.0, 0.0).astype(BF16)


def pick(matrix, rows):
    return lax.dot_general(matrix, rows, (((1,), (0,)), ((), ())), preferred_element_type=F32)


def pack_matrix(code_row, at, shift, sizes):
    places, samples, sections, capacity = sizes
    row_place, row_slot = split(iota2((places * capacity, places * samples), 0), capacity)
    col_place, _ = split(iota2((1, places * samples), 1), samples)
    target = lax.rem(at + shift, sections)
    return one_hot((row_place == col_place) & (code_row == target * capacity + row_slot))


def first_pack_kernel(path_ref, at_ref, maps_ref, *refs, sizes):
    places, samples, sections, capacity = sizes
    out_refs, code_ref = refs[:-1], refs[-1]
    codes = slot_codes(path_ref, samples, capacity)
    _, col_sample = split(iota2((1, places * samples), 1), samples)
    code_row = spread_codes(codes, col_sample)
    for shift in range(1, sections):
        matrix = pack_matrix(code_row, at_ref[0], shift, sizes)
        out_refs[shift - 1][...] = pick(matrix, maps_ref[...]).astype(BF16)
    code_ref[...] = jnp.broadcast_to(code_row, code_ref.shape)


def second_pack_kernel(code_ref, at_ref, maps_ref, *out_refs, sizes):
    _, _, sections, _ = sizes
    for shift in range(1, sections):
        matrix = pack_matrix(code_ref[:1, :], at_ref[0], shift, sizes)
        out_refs[shift - 1][...] = pick(matrix, maps_ref[...]).astype(BF16)


def prepare_kernel(path_ref, at_ref, code_ref, maps_ref, grads_ref, kernel_ref, *refs, sizes):
    places, samples, sections, capacity = sizes
    slots = sections * capacity
    own_maps_ref, own_grads_ref, taps_ref, place_ref, fetch_ref, home_ref, merge_ref = refs
    row_place, row_slot = split(iota2((places * slots, places * samples), 0), slots)
    col_place, _ = split(iota2((1, places * samples), 1), samples)
    mask = (
        (row_place == col_place)
        & (row_slot < capacity)
        & (code_ref[:1, :] == at_ref[0] * capacity + row_slot)
    )
    matrix = one_hot(mask)
    own_maps_ref[...] = pick(matrix, maps_ref[...]).astype(BF16)
    own_grads_ref[...] = pick(matrix, grads_ref[...]).astype(BF16)
    kind = lax.rem(at_ref[0], 3)
    for tap in range(25):
        taps_ref[tap] = kernel_ref[tap] * tap_keep(kind, tap)

    row_place, row_slot = split(iota2((places * slots, places * capacity), 0), slots)
    col_place, col_slot = split(iota2((1, places * capacity), 1), capacity)
    for shift in range(1, sections):
        mask = (row_place == col_place) & (row_slot == shift * capacity + col_slot)
        place_ref[shift - 1] = one_hot(mask)
    row_place, row_slot = split(iota2((places * capacity, places * slots), 0), capacity)
    col_place, col_slot = split(iota2((1, places * slots), 1), slots)
    for shift in range(1, sections):
        mask = (row_place == col_place) & (col_slot == shift * capacity + row_slot)
        fetch_ref[shift - 1] = one_hot(mask)

    codes = slot_codes(path_ref, samples, capacity)
    row_place, row_sample = split(iota2((places * samples, 1), 0), samples)
    row_code = spread_codes(codes, row_sample)
    col_place, col_slot = split(iota2((1, places * slots), 1), slots)
    mask = (
        (row_place == col_place)
        & (col_slot < capacity)
        & (row_code == at_ref[0] * capacity + col_slot)
    )
    home_ref[...] = one_hot(mask)
    col_place, col_slot = split(iota2((1, places * capacity), 1), capacity)
    for shift in range(1, sections):
        target = lax.rem(at_ref[0] + shift, sections)
        mask = (row_place == col_place) & (row_code == target * capacity + col_slot)
        merge_ref[shift - 1] = one_hot(mask)


def gather_slots(own_ref, place_ref, got_refs):
    total = own_ref[...].astype(F32)
    for at, got_ref in enumerate(got_refs):
        total = total + pick(place_ref[at], got_ref[...])
    return total


def return_slots(slot_rows, fetch_ref, out_refs):
    for at, out_ref in enumerate(out_refs):
        out_ref[...] = pick(fetch_ref[at], slot_rows).astype(BF16)


def unpack_kernel(home_ref, merge_ref, slots_ref, *refs):
    got_refs, out_ref = refs[:-1], refs[-1]
    total = pick(home_ref[...], slots_ref[...])
    for at, got_ref in enumerate(got_refs):
        total = total + pick(merge_ref[at], got_ref[...])
    out_ref[...] = total.astype(BF16)


def tap_keep(kind, tap):
    row_shift, col_shift = tap // 5 - 2, tap % 5 - 2
    narrow = abs(row_shift) <= 1 and abs(col_shift) <= 1
    spaced = row_shift % 2 == 0 and col_shift % 2 == 0
    keep = kind == 1
    if narrow:
        keep = keep | (kind == 0)
    if spaced:
        keep = keep | (kind == 2)
    return jnp.where(keep, 1.0, 0.0).astype(F32)


def correlate(source_ref, kernel_ref, side, slots, sign, emit):
    channels = source_ref.shape[-1]

    def chunk(at, carry):
        lanes = pl.ds(pl.multiple_of(at * LANES, LANES), LANES)
        taps = [
            jnp.broadcast_to(kernel_ref[tap, :, lanes], (slots, LANES)) for tap in range(25)
        ]
        for row in range(side):
            sums = [None] * side
            for row_shift in range(-2, 3):
                source_row = row + sign * row_shift
                if not 0 <= source_row < side:
                    continue
                cells = [
                    source_ref[pl.ds((source_row * side + col) * slots, slots), lanes]
                    for col in range(side)
                ]
                for col_shift in range(-2, 3):
                    tap = taps[(row_shift + 2) * 5 + col_shift + 2]
                    for col in range(side):
                        source_col = col + sign * col_shift
                        if not 0 <= source_col < side:
                            continue
                        term = tap * cells[source_col]
                        sums[col] = term if sums[col] is None else sums[col] + term
            for col in range(side):
                emit(pl.ds((row * side + col) * slots, slots), lanes, sums[col])
        return carry

    lax.fori_loop(0, channels // LANES, chunk, 0)


def deal(replica_ref, rows_ref, give_ref, hold_ref):
    low = replica_ref[0] & 1
    count, block = give_ref.shape[0], give_ref.shape[1]
    for at in range(count):
        give_ref[at] = rows_ref[pl.ds(pl.multiple_of((2 * at + 1 - low) * block, block), block), :]
        hold_ref[at] = rows_ref[pl.ds(pl.multiple_of((2 * at + low) * block, block), block), :]


def forward_kernel(replica_ref, own_ref, place_ref, fetch_ref, weight_ref, kernel_ref, *refs, sizes, side):
    _, _, sections, capacity = sizes
    slots = sections * capacity
    got_refs, refs = refs[: sections - 1], refs[sections - 1 :]
    back_refs, refs = refs[: sections - 1], refs[sections - 1 :]
    give_refs, refs = refs[: sections - 1], refs[sections - 1 :]
    hold_refs, refs = refs[: sections - 1], refs[sections - 1 :]
    final_ref, active_ref, scaled_ref, inverse_ref, source_ref, turned_ref = refs
    source_ref[...] = gather_slots(own_ref, place_ref, got_refs)

    def emit(rows, lanes, value):
        scaled_ref[rows, lanes] = value

    correlate(source_ref, kernel_ref, side, slots, 1, emit)
    block = side * slots
    for row in range(side):
        rows = pl.ds(row * block, block)
        mixed = scaled_ref[rows, :]
        inverse = lax.rsqrt(jnp.mean(mixed * mixed, axis=-1, keepdims=True) + EPS)
        scaled = mixed * inverse
        scaled_ref[rows, :] = scaled
        inverse_ref[rows, :] = jnp.broadcast_to(inverse, (block, LANES))
        active_ref[rows, :] = (scaled * jax.nn.sigmoid(scaled)).astype(BF16)
    branch = pick(active_ref[...], weight_ref[...])
    final_ref[...] = (source_ref[...] + branch).astype(BF16)
    return_slots(final_ref[...], fetch_ref, back_refs)
    for at in range(sections - 1):
        turned = lax.dot_general(
            active_ref[...], fetch_ref[at], (((0,), (1,)), ((), ())), preferred_element_type=F32
        )
        turned_ref[...] = turned.astype(BF16)
        deal(replica_ref, turned_ref, give_refs[at], hold_refs[at])


def own_point_kernel(active_ref, own_ref, total_ref):
    total = lax.dot_general(
        active_ref[...], own_ref[...], (((0,), (0,)), ((), ())), preferred_element_type=F32
    )
    total_ref[...] = total.reshape(total_ref.shape)


def point_kernel(replica_ref, own_ref, *refs, flip):
    out_ref = refs[-1]
    active_refs, got_refs = refs[: len(refs) // 2], refs[len(refs) // 2 : -1]
    count, block, _ = out_ref.shape
    total = None
    for active_ref, got_ref in zip(active_refs, got_refs):
        active = active_ref[...].reshape(count * block, active_ref.shape[2])
        share = pick(active, got_ref[...])
        total = share if total is None else total + share
    total = total.reshape(out_ref.shape)
    which = (replica_ref[0] & 1) ^ flip
    for at in range(count):
        out_ref[at] = (total[at] + own_ref[2 * at + which]).astype(out_ref.dtype)


def fold_kernel(replica_ref, keep_ref, got_ref, send_ref, left_ref, *, strides, bits):
    core = replica_ref[0] & 1
    mine = jnp.where(core == 0, (replica_ref[0] // bits[0]) & 1, (replica_ref[0] // bits[1]) & 1)
    for at in range(send_ref.shape[0]):
        low, high = [(at // stride) * 2 * stride + at % stride for stride in strides]
        base = jnp.where(core == 0, low, high)
        step = jnp.where(core == 0, strides[0], strides[1])
        give = base + step * (1 - mine)
        hold = base + step * mine
        send_ref[at] = (keep_ref[give] + got_ref[give].astype(F32)).astype(BF16)
        left_ref[at] = keep_ref[hold] + got_ref[hold].astype(F32)


def last_kernel(replica_ref, keep_ref, got_ref, taps_ref, came_ref, point_ref, out_ref):
    point_ref[...] = keep_ref[0] + got_ref[0].astype(F32)
    core = replica_ref[0] & 1
    half = taps_ref.shape[-1]
    out_ref[:, :, pl.ds(pl.multiple_of(core * half, LANES), half)] = taps_ref[...]
    out_ref[:, :, pl.ds(pl.multiple_of((1 - core) * half, LANES), half)] = came_ref[...]


def mixed_kernel(own_ref, place_ref, weight_ref, scaled_ref, inverse_ref, *refs, block):
    got_refs, (slot_grads_ref, mixed_ref, work_ref) = refs[:-3], refs[-3:]
    slot_grads_ref[...] = gather_slots(own_ref, place_ref, got_refs).astype(BF16)
    work_ref[...] = lax.dot_general(
        slot_grads_ref[...], weight_ref[...], (((1,), (1,)), ((), ())), preferred_element_type=F32
    )
    for at in range(0, work_ref.shape[0], block):
        rows = pl.ds(at, block)
        scaled = scaled_ref[rows, :]
        logistic = jax.nn.sigmoid(scaled)
        grad_scaled = work_ref[rows, :] * logistic * (1.0 + scaled * (1.0 - logistic))
        mean = jnp.mean(grad_scaled * scaled, axis=-1, keepdims=True)
        mixed_ref[rows, :] = inverse_ref[rows, :1] * (grad_scaled - scaled * mean)


def backward_kernel(slot_grads_ref, fetch_ref, kernel_ref, mixed_ref, *refs, side, slots):
    back_refs, grad_in_ref, work_ref = refs[:-2], refs[-2], refs[-1]

    def emit(rows, lanes, value):
        work_ref[rows, lanes] = value

    correlate(mixed_ref, kernel_ref, side, slots, -1, emit)
    grad_in_ref[...] = (slot_grads_ref[...].astype(F32) + work_ref[...]).astype(BF16)
    return_slots(grad_in_ref[...], fetch_ref, back_refs)


def taps_kernel(at_ref, replica_ref, mixed_ref, source_ref, out_ref, *, side, slots, flip):
    kind = lax.rem(at_ref[0], 3)
    half = out_ref.shape[-1]
    which = (replica_ref[0] & 1) ^ flip

    def chunk(at, carry):
        lanes = pl.ds(pl.multiple_of(which * half + at * LANES, LANES), LANES)
        target = pl.ds(pl.multiple_of(at * LANES, LANES), LANES)

        def cells(ref, row):
            return [ref[pl.ds((row * side + col) * slots, slots), lanes] for col in range(side)]

        sums = [None] * 25
        for row in range(side):
            grads = cells(mixed_ref, row)
            for row_shift in range(-2, 3):
                if not 0 <= row + row_shift < side:
                    continue
                source = cells(source_ref, row + row_shift)
                for col_shift in range(-2, 3):
                    tap = (row_shift + 2) * 5 + col_shift + 2
                    terms = [
                        grads[col] * source[col + col_shift]
                        for col in range(side)
                        if 0 <= col + col_shift < side
                    ]
                    while len(terms) > 1:
                        terms = [sum(terms[i + 1 : i + 2], terms[i]) for i in range(0, len(terms), 2)]
                    sums[tap] = terms[0] if sums[tap] is None else sums[tap] + terms[0]
        for tap in range(25):
            out_ref[tap, :, target] = (
                jnp.sum(sums[tap], axis=0, keepdims=True) * tap_keep(kind, tap)
            )
        return carry

    lax.fori_loop(0, half // LANES, chunk, 0)


def call(kernel, outs, in_specs, scratch=(), megabytes=20):
    return pl.pallas_call(
        kernel,
        out_shape=outs,
        in_specs=in_specs,
        out_specs=jax.tree.map(lambda _: VMEM, outs),
        scratch_shapes=list(scratch),
        compiler_params=pltpu.CompilerParams(vmem_limit_bytes=megabytes * 1024 * 1024),
    )


def window(feature_maps, path_lists, point_weight, depth_kernel, cotangent):
    sections = lax.axis_size("segment")
    ways = lax.axis_size("rep")
    at = lax.axis_index("segment").astype(jnp.int32).reshape(1)
    replica = lax.axis_index("rep").astype(jnp.int32).reshape(1)
    samples, side, _, channels = feature_maps.shape
    places = side * side
    capacity = max(max(2, samples // 4), (samples + sections - 1) // sections)
    slots = sections * capacity
    sizes = (places, samples, sections, capacity)
    path = path_lists[0, :, 0]
    weight = point_weight[0, 0]
    kernel = depth_kernel[0, 0].reshape(25, 1, channels)
    others = range(1, sections)

    def rows_of(maps):
        return jnp.transpose(maps, (1, 2, 0, 3)).reshape(places * samples, channels)

    def maps_of(rows):
        return jnp.transpose(rows.reshape(side, side, samples, channels), (2, 0, 1, 3))

    def shape(*dims, dtype=F32):
        return jax.ShapeDtypeStruct(dims, dtype)

    packed = shape(places * capacity, channels, dtype=BF16)

    def swap(pieces, direction):
        return [
            lax.ppermute(
                piece,
                "segment",
                [(i, (i + direction * shift) % sections) for i in range(sections)],
            )
            for shift, piece in zip(others, pieces)
        ]

    def unpack(slot_rows, pieces):
        return call(
            unpack_kernel, shape(places * samples, channels, dtype=BF16), [VMEM] * (3 + len(pieces))
        )(home, merge, slot_rows, *pieces)

    def trade(value, pair):
        return lax.ppermute(value, "rep", [(i, i ^ pair[i & 1]) for i in range(ways)])

    maps, grads = rows_of(feature_maps), rows_of(cotangent)
    code_shape = jax.ShapeDtypeStruct((8, places * samples), jnp.int32)
    *packs, code_row = call(
        functools.partial(first_pack_kernel, sizes=sizes),
        [packed for _ in others] + [code_shape],
        [SMEM, SMEM, VMEM],
        megabytes=56,
    )(path, at, maps)
    got_maps = swap(packs, 1)
    packs = call(
        functools.partial(second_pack_kernel, sizes=sizes),
        [packed for _ in others],
        [VMEM, SMEM, VMEM],
    )(code_row, at, grads)
    got_grads = swap(packs, 1)

    slot_shape = shape(places * slots, channels)
    slot_half = shape(places * slots, channels, dtype=BF16)
    tap_shape = shape(25, 1, channels)
    own_maps, own_grads, kernel, place, fetch, home, merge = call(
        functools.partial(prepare_kernel, sizes=sizes),
        [
            slot_half,
            slot_half,
            tap_shape,
            shape(sections - 1, places * slots, places * capacity, dtype=BF16),
            shape(sections - 1, places * capacity, places * slots, dtype=BF16),
            shape(places * samples, places * slots, dtype=BF16),
            shape(sections - 1, places * samples, places * capacity, dtype=BF16),
        ],
        [SMEM, SMEM, VMEM, VMEM, VMEM, VMEM],
    )(path, at, code_row, maps, grads, kernel)
    block = channels // ways
    turned = shape(ways // 2, block, places * capacity, dtype=BF16)
    results = call(
        functools.partial(forward_kernel, sizes=sizes, side=side),
        [packed for _ in others]
        + [turned for _ in others] * 2
        + [slot_half, slot_half, slot_shape, shape(places * slots, LANES), slot_shape],
        [SMEM] + [VMEM] * (5 + len(got_maps)),
        [pltpu.VMEM((channels, places * capacity), BF16)],
    )(replica, own_maps, place, fetch, weight, kernel, *got_maps)
    count = sections - 1
    back, active_give, active_hold = [results[i * count : (i + 1) * count] for i in range(3)]
    slot_final, active, scaled, inverse, source = results[3 * count :]

    part = shape(ways // 2, block, channels)
    own_point = call(
        own_point_kernel, shape(ways, block, channels), [VMEM, VMEM]
    )(active, own_grads)
    got_final = swap(back, -1)

    def point(flip, out, active_blocks):
        return call(
            functools.partial(point_kernel, flip=flip), out, [SMEM] + [VMEM] * (1 + 2 * count)
        )(replica, own_point, *active_blocks, *got_grads)

    send = point(1, shape(*part.shape, dtype=BF16), active_give)
    got = trade(send, (1, 1))
    keep = point(0, part, active_hold)

    slot_grads, mixed = call(
        functools.partial(mixed_kernel, block=side * slots),
        [slot_half, slot_shape],
        [VMEM] * (5 + len(got_grads)),
        [pltpu.VMEM((places * slots, channels), F32)],
    )(own_grads, place, weight, scaled, inverse, *got_grads)
    *back, slot_in = call(
        functools.partial(backward_kernel, side=side, slots=slots),
        [packed for _ in others] + [slot_half],
        [VMEM] * 4,
        [pltpu.VMEM((places * slots, channels), F32)],
    )(slot_grads, fetch, kernel, mixed)
    got_in = swap(back, -1)

    half_shape = shape(25, 1, channels // 2)

    def tap_sums(flip):
        return call(
            functools.partial(taps_kernel, side=side, slots=slots, flip=flip),
            half_shape,
            [SMEM, SMEM, VMEM, VMEM],
        )(at, replica, mixed, source)

    give, taps = tap_sums(1), tap_sums(0)

    bits = [1 << i for i in range(1, ways.bit_length() - 1)]
    swapped = bits[1::-1] + bits[2:] if len(bits) > 2 else bits
    for step, pair in enumerate(zip(bits, swapped)):
        count = (ways // 4) >> step
        strides = []
        for order in (bits, swapped):
            done = order[:step]
            strides.append(1 << sum(1 for other in bits if other < order[step] and other not in done))
        send, keep = call(
            functools.partial(fold_kernel, strides=strides, bits=pair),
            [shape(count, block, channels, dtype=BF16), shape(count, block, channels)],
            [SMEM, VMEM, VMEM],
        )(replica, keep, got)
        got = trade(send, pair)

    later = bits[:-1]
    pairs = [(1, 1), (bits[-1], bits[-1])] + list(zip(later, later[1:] + later[:1]))
    for step, pair in enumerate(pairs):
        came = trade(give if step == 0 else taps, pair)
        taps = taps + came
    came = trade(taps, (1, 1))
    point_grad, taps = call(
        last_kernel, [shape(block, channels), tap_shape], [SMEM] + [VMEM] * 4
    )(replica, keep, got, taps, came)

    final_maps = maps_of(unpack(slot_final, got_final))
    input_grad = maps_of(unpack(slot_in, got_in))
    return (
        final_maps,
        input_grad,
        point_grad.reshape(1, 1, block, channels),
        taps.reshape(1, 1, 25, channels),
    )


def solution(mesh):
    placed = (
        P(("segment", "rep"), None, None, None),
        P(None, ("segment", "rep"), None),
        P(None, "segment", None, None),
        P(None, "segment", None, None),
        P(("segment", "rep"), None, None, None),
    )
    return jax.shard_map(
        window,
        mesh=mesh,
        in_specs=placed,
        out_specs=(
            P(("segment", "rep"), None, None, None),
            P(("segment", "rep"), None, None, None),
            P(None, "segment", "rep", None),
            P(None, "segment", None, None),
        ),
        check_vma=False,
    )
```
